32 devices in a mesh: groups: 2 (over y), slab: 4 (over z), pair: 4 (over x, core).
Axes of the slice: x: 2, y: 2, z: 4, core: 2. Of those that a mesh axis runs over, the one named last changes fastest.
Arguments:
- occupancy: float32 [8, 128, 256, 128], P(('groups', 'pair'), 'slab'), parts along dimension 0, may hold values from 0 to 1
- classes: int32 [8, 128, 256, 128], P(('groups', 'pair'), 'slab'), parts along dimension 0, may hold values from 0 to 7
- conductance: float32 [8], replicated, may hold values from 0.1 to 1
- damping: float32 [8], P('groups'), parts along dimension 0, may hold values from 1 to 8
- matches: int32 [8], P('groups'), parts along dimension 0, may hold values from 0 to 3, each once
Outputs:
- correlation: float32 [8, 128, 256, 128], P(('groups', 'pair'), 'slab'), parts along dimension 0
The draws below stay inside these ranges and needn't reach their ends.
There are 2 independent parts, one for each index of `groups`. The reference program is written for one: setup_inputs(seed, part) draws one part's arguments, and reference() takes and returns one part's arrays. A program takes and returns all parts, laid end to end along the dimension named above; an argument that names none is the same for every part. Nothing has to cross between parts.
Inputs may be any that keep to these rules, and one draw needn't show every extreme that they name: A permutation of the 4 submaps; submap s is registered against submap matches[s]. `classes`: a row of the conductance table.
All inputs are finite; a program needn't handle non-finite values.
Results may differ from the reference program's by a relative error of at most 0.0003.
Values sent between devices are 32-bit elements; how exact they have to be, the bound alone decides.
No kernel may reach another device: no remote copies, remote signals or barrier semaphores. Data moves between devices by JAX's collectives and lax.ppermute only.
A program may use at most 128 MiB of HBM per device.

```python
import math
import jax
import jax.numpy as jnp
from jax import lax

X = 256
Y = 128
Z = 128
STEPS = 4
NCLASS = 8
SUBMAPS = 4


def touch_ends(entries, key, smallest, largest):
    place = [jax.random.randint(jax.random.fold_in(key, axis), (), 0, length) for axis, length in enumerate(entries.shape)]
    widest = entries.shape.index(max(entries.shape))
    next_to = place[:widest] + [(place[widest] + 1) % entries.shape[widest]] + place[widest + 1:]
    return entries.at[tuple(place)].set(smallest).at[tuple(next_to)].set(largest)


def shard_levels(stream_key, extent, pieces, smallest, largest):
    def one(dim, shards_of):
        draws = jax.random.uniform(jax.random.fold_in(jax.random.fold_in(stream_key, 6), dim), (shards_of,), jnp.float32, smallest / len(pieces), largest / len(pieces))
        return jnp.repeat(jnp.exp(draws), extent[dim] // shards_of).reshape((-1,) + (1,) * (len(extent) - dim - 1))

    loudness = one(*pieces[0])
    for cut in pieces[1:]:
        loudness = loudness * one(*cut)
    return loudness


def setup_inputs(seed: int = 0, part: int = 0) -> dict:
    splits = jax.random.split(jax.random.key(seed), 6)
    own_keys = jax.random.split(jax.random.fold_in(splits[5], part), 6)
    occupancy = jnp.clip(1.0 * jax.random.uniform(own_keys[0], (SUBMAPS, Z, X, Y), jnp.float32) ** shard_levels(own_keys[0], (SUBMAPS, Z, X, Y), ((0, 4), (1, 4)), -0.2, 0.2), 0.0, 1.0)
    classes = touch_ends(jax.random.randint(own_keys[1], (SUBMAPS, Z, X, Y), 0, NCLASS), jax.random.fold_in(own_keys[1], 1), 0, NCLASS - 1).astype(jnp.int32)
    conductance = jnp.clip(jnp.exp(jax.random.uniform(splits[2], (NCLASS,), jnp.float32, math.log(0.1), math.log(1.0))), 0.1, 1.0)
    damping = jnp.clip(jnp.exp(jax.random.uniform(own_keys[3], (SUBMAPS,), jnp.float32, math.log(1.0), math.log(8.0))), 1.0, 8.0)
    matches = jax.random.permutation(own_keys[4], SUBMAPS).astype(jnp.int32)
    return {"occupancy": occupancy, "classes": classes, "conductance": conductance, "damping": damping, "matches": matches}


STEP_SIZE = 1.0 / 6.0
FLOOR_VALUE = 0.01

def neighbours(padded):
    return [padded[2:, 1:-1, 1:-1], padded[:-2, 1:-1, 1:-1], padded[1:-1, 2:, 1:-1], padded[1:-1, :-2, 1:-1], padded[1:-1, 1:-1, 2:], padded[1:-1, 1:-1, :-2]]

def diffuse(volume, conduct):
    outer_rims = neighbours(jnp.pad(conduct, 1))
    for sweep_index in range(STEPS):
        beside_all = neighbours(jnp.pad(volume, 1))
        change = jnp.zeros_like(volume)
        for other_field, other_conduct in zip(beside_all, outer_rims):
            change = change + 0.5 * (conduct + other_conduct) * (other_field - volume)
        volume = volume + STEP_SIZE * change
    return volume

def frequency(length):
    counter = jnp.arange(length, dtype=jnp.int32)
    return (jnp.where(counter < length // 2, counter, counter - length) / length).astype(jnp.float32)

def reference(occupancy, classes, conductance, damping, matches):

    def spectrum(inputs):
        volume, labels = inputs
        smooth = diffuse(volume, conductance[labels])
        transformed = jnp.fft.fftn(smooth, norm='ortho')
        return (jnp.real(transformed), jnp.imag(transformed))
    real_part, imag_part = lax.map(spectrum, (occupancy, classes))
    radius = frequency(Z)[:, None, None] ** 2 + frequency(X)[None, :, None] ** 2 + frequency(Y)[None, None, :] ** 2

    def correlate(position):
        partner = matches[position]
        own_real = real_part[position]
        own_imag = imag_part[position]
        far_real = real_part[partner]
        far_imag = imag_part[partner]
        cross_real = own_real * far_real + own_imag * far_imag
        cross_imag = own_imag * far_real - own_real * far_imag
        magnitude = jnp.sqrt((own_real ** 2 + own_imag ** 2) * (far_real ** 2 + far_imag ** 2) + FLOOR_VALUE ** 2)
        weight = jnp.exp(-damping[position] * radius) / magnitude
        inverse = jnp.fft.ifftn(lax.complex(cross_real * weight, cross_imag * weight), norm='ortho')
        return jnp.real(inverse).astype(jnp.float32)
    return lax.map(correlate, jnp.arange(SUBMAPS, dtype=jnp.int32))
```

```python
import functools
import math

import jax
import jax.numpy as jnp
import ml_dtypes
import numpy as np
from jax import lax
from jax.experimental import pallas as pl
from jax.experimental.pallas import tpu as pltpu
from jax.sharding import PartitionSpec as P

STEPS = 4
STEP_SIZE = 1.0 / 6.0
FLOOR_VALUE = 0.01
AXES = ("slab", "pair")
PAD = 8
VMEM_BYTES = 60 * 1024 * 1024
BF = jnp.bfloat16
F32 = jnp.float32


def split_table(table):
    high = table.astype(ml_dtypes.bfloat16)
    low = (table - high.astype(np.float64)).astype(ml_dtypes.bfloat16)
    return high, low


def trig(rows, columns, length):
    angles = (np.asarray(rows)[:, None] * np.asarray(columns)[None, :] % length) * (2.0 * math.pi / length)
    factor = 1.0 / math.sqrt(length)
    return np.cos(angles) * factor, np.sin(angles) * factor


def left_table(table):
    high, low = split_table(table)
    return np.concatenate([high, high, low], axis=1)


def right_table(table):
    high, low = split_table(table)
    top = np.concatenate([high, low], axis=1)
    return np.concatenate([top, np.concatenate([high, np.zeros_like(low)], axis=1)], axis=0)


def half_forward(length):
    half = length // 2
    cosine, sine = trig(np.arange(length), np.arange(half + 1), length)
    return np.concatenate([cosine[:, :half], cosine[:, half:], -sine[:, 1:half]], axis=1)


def half_inverse(length):
    half = length // 2
    cosine, sine = trig(np.arange(half + 1), np.arange(length), length)
    return np.concatenate(
        [cosine[:1], 2 * cosine[1:half], cosine[half:], -2 * sine[1:half]], axis=0
    )


def first_column_masks(rows, length, lanes):
    half = lanes // 2
    lower = (rows > 0) & (rows < length // 2)
    upper = rows > length // 2
    sign = np.where(np.arange(lanes) < half, 1.0, -1.0)
    take_cosine = np.ones((rows.size, lanes))
    take_sine = np.ones((rows.size, lanes)) * sign
    take_sine[lower, 0] = 0
    take_cosine[lower, half] = 0
    take_cosine[upper, 0] = 0
    take_sine[upper, half] = 0
    weight = np.ones((rows.size, lanes))
    weight[lower, 0] = 2
    weight[lower, half] = 0
    weight[upper, 0] = 0
    weight[upper, half] = 2
    return take_cosine.astype(np.float32), take_sine.astype(np.float32), weight.astype(np.float32)


def split(values):
    high = values.astype(BF)
    return high, (values - high.astype(F32)).astype(BF)


def dot(a, b):
    return jnp.dot(a, b, preferred_element_type=F32)


def along_lanes(values, table):
    high, low = split(values)
    both = dot(jnp.concatenate([high, low], axis=1), table)
    lanes = values.shape[1]
    return both[:, :lanes] + both[:, lanes:]


def forward_kernel(steps, chunks, depth, *refs):
    if steps:
        occ, cls, below, above, edge, conductance = refs[:6]
        refs = refs[6:]
    else:
        occ = refs[0]
        refs = refs[1:]
    table_y, table_x, take_cosine, take_sine = refs[:4]
    outs = refs[4 : 4 + chunks]
    scratch = refs[4 + chunks :]
    length, lanes = occ.shape[1:]
    rows = length // chunks
    if steps:
        first, second, centre, along_x, along_y, along_z = scratch
        total = depth + 2 * steps
        lane = lax.broadcasted_iota(jnp.int32, (length, lanes), 1)
        zeros = jnp.zeros((PAD, lanes), F32)
        inside = pl.ds(PAD, length)
        kappa = second

        def fill(z, ids, field):
            value = jnp.zeros((length, lanes), F32)
            for index in range(conductance.shape[0]):
                value = jnp.where(ids == index, conductance[index] * (0.5 * STEP_SIZE), value)
            kappa[z, inside, :] = value
            first[z, inside, :] = field

        def clear(z, carry):
            for ref in (first, second, along_x):
                ref[z, pl.ds(0, PAD), :] = zeros
                ref[z, pl.ds(PAD + length, PAD), :] = zeros
            return carry

        lax.fori_loop(0, total, clear, 0)

        def own(z, carry):
            fill(z + steps, cls[z], occ[z])
            return carry

        lax.fori_loop(0, depth, own, 0)

        def outer(z, carry):
            for ref, start, flag in ((below, 0, 0), (above, steps + depth, 1)):
                fill(start + z, ref[steps + z].astype(jnp.int32), ref[z])

                @pl.when(edge[flag] == 0)
                def _():
                    kappa[start + z, inside, :] = jnp.zeros((length, lanes), F32)

            return carry

        lax.fori_loop(0, steps, outer, 0)

        block = 64

        def coefficients(z, carry):
            for x in range(0, length, block):
                here = kappa[z, pl.ds(PAD + x, block), :]
                x_next = kappa[z, pl.ds(PAD + x + 1, block), :]
                x_back = kappa[z, pl.ds(PAD + x - 1, block), :]
                z_next = kappa[z + 1, pl.ds(PAD + x, block), :]
                z_back = kappa[z - 1, pl.ds(PAD + x, block), :]
                at = lane[x : x + block]
                y_next = jnp.where(at < lanes - 1, pltpu.roll(here, lanes - 1, 1), 0.0)
                y_back = jnp.where(at > 0, pltpu.roll(here, 1, 1), 0.0)
                along_x[z, pl.ds(PAD + x, block), :] = here + x_next
                along_y[z, pl.ds(x, block), :] = jnp.where(at < lanes - 1, here + y_next, 0.0)
                along_z[z, pl.ds(x, block), :] = here + z_next
                around = (x_next + x_back) + (y_next + y_back) + (z_next + z_back)
                centre[z, pl.ds(x, block), :] = 1.0 - (6.0 * here + around)
            return carry

        lax.fori_loop(1, total - 1, coefficients, 0)

        def first_faces(x, carry):
            along_z[0, pl.ds(x * PAD, PAD), :] = (
                kappa[0, pl.ds(PAD + x * PAD, PAD), :] + kappa[1, pl.ds(PAD + x * PAD, PAD), :]
            )
            return carry

        lax.fori_loop(0, length // PAD, first_faces, 0)

        old, new = first, second
        for step in range(1, steps + 1):

            def advance(z, carry):
                scale = jnp.where(
                    ((z < steps) & (edge[0] == 0)) | ((z >= steps + depth) & (edge[1] == 0)), 0.0, 1.0
                )
                for x in range(0, length, block):
                    own_rows = pl.ds(x, block)
                    padded_rows = pl.ds(PAD + x, block)
                    here = old[z, padded_rows, :]
                    face_y = along_y[z, own_rows, :]
                    value = centre[z, own_rows, :] * here
                    value += face_y * pltpu.roll(here, lanes - 1, 1)
                    value += pltpu.roll(face_y * here, 1, 1)
                    value += along_x[z, padded_rows, :] * old[z, pl.ds(PAD + x + 1, block), :]
                    back = pl.ds(PAD + x - 1, block)
                    value += along_x[z, back, :] * old[z, back, :]
                    value += along_z[z, own_rows, :] * old[z + 1, padded_rows, :]
                    value += along_z[z - 1, own_rows, :] * old[z - 1, padded_rows, :]
                    new[z, padded_rows, :] = value * scale
                return carry

            lax.fori_loop(step, total - step, advance, 0)
            old, new = new, old
        plane = lambda z: old[z + steps, pl.ds(PAD, length), :]
    else:
        plane = lambda z: occ[z]

    width = 2

    def transform(group, carry):
        sides = []
        for k in range(width):
            sides.append(along_lanes(plane(group * width + k), table_y[...]))
        high, low = split(jnp.concatenate(sides, axis=1))
        both = dot(table_x[...], jnp.concatenate([high, low, high], axis=0))
        for k in range(width):
            part = both[:, k * lanes : (k + 1) * lanes]
            turned = pltpu.roll(part[length:], lanes // 2, 1)
            value = take_cosine[...] * part[:length] + take_sine[...] * turned
            for chunk in range(chunks):
                outs[chunk][pl.ds(group * width + k, rows, stride=depth), :] = value[
                    chunk * rows : (chunk + 1) * rows
                ]
        return carry

    lax.fori_loop(0, depth // width, transform, 0)


def cross_kernel(length_x, start, damping, matches, spectra, table_f, table_i, out, held, weight):
    slabs, submaps, _, depth, lanes = spectra.shape
    length_z = slabs * depth
    half = lanes // 2
    lane = lax.broadcasted_iota(jnp.int32, (length_z, lanes), 1)
    sign = jnp.where(lane < half, 1.0, -1.0)
    first = (lane == 0) | (lane == half)
    row = start[0] + pl.program_id(0)
    special = (row == 0) | (row == length_x // 2)
    upper = row > length_x // 2

    def signed(count, length):
        return jnp.where(count < length // 2, count, count - length).astype(F32) / length

    @pl.when(pl.program_id(0) == 0)
    def _():
        along = signed(lax.broadcasted_iota(jnp.int32, (length_z, lanes), 0), length_z)
        for s in range(submaps):
            weight[s] = jnp.exp(-damping[s] * (along * along))

    at_x = signed(row, length_x)
    lane_row = lax.broadcasted_iota(jnp.int32, (8, lanes), 1)
    count_y = jnp.where(lane_row < half, lane_row, lane_row - half)
    nyquist = ((lane_row == 0) & upper) | ((lane_row == half) & (special | upper))
    at_y = jnp.where(nyquist, -0.5, signed(count_y, lanes))
    radius = at_x * at_x + at_y * at_y

    for s in range(submaps):
        column = jnp.concatenate([spectra[i, s, 0] for i in range(slabs)], axis=0)
        high, low = split(column)
        both = dot(table_f[...], jnp.concatenate([high, low, high], axis=0))
        cosine, sine = both[:length_z], both[length_z:]
        value = cosine + sign * pltpu.roll(sine, half, 1)
        square = value * value
        held[0, s] = value
        held[1, s] = square + pltpu.roll(square, half, 1)
        held[2, s] = cosine
        held[3, s] = sine

    for s in range(submaps):
        partner = matches[s]
        own, far = held[0, s], held[0, partner]
        damp = weight[s] * jnp.tile(jnp.exp(-damping[s] * radius), (length_z // 8, 1))
        scale = damp * lax.rsqrt(held[1, s] * held[1, partner] + FLOOR_VALUE**2)
        same = own * far
        mixed = own * pltpu.roll(far, half, 1)
        real = same + pltpu.roll(same, half, 1)
        imag = mixed - pltpu.roll(mixed, half, 1)
        imag = jnp.where(lane < half, -imag, imag)
        x_here = jnp.where(lane < half, real, imag) * scale
        x_turn = jnp.where(lane < half, -imag, real) * scale
        held[4, s] = jnp.where(first & upper, x_turn, x_here)
        held[5, s] = jnp.where(first & upper, -x_here, x_turn)

        @pl.when(special)
        def _():
            own_r, own_i = held[2, s], -held[3, s]
            far_r, far_i = held[2, partner], -held[3, partner]
            size = (own_r * own_r + own_i * own_i) * (far_r * far_r + far_i * far_i)
            scale = damp * lax.rsqrt(size + FLOOR_VALUE**2)
            held[4, s] = jnp.where(first, (own_r * far_r + own_i * far_i) * scale, held[4, s])
            held[5, s] = jnp.where(first, (own_r * far_i - own_i * far_r) * scale, held[5, s])

        high, low = split(jnp.concatenate([held[4, s], held[5, s]], axis=0))
        back = dot(table_i[...], jnp.concatenate([high, low, high], axis=0))
        for i in range(slabs):
            out[i, s, 0] = back[i * depth : (i + 1) * depth]


def inverse_kernel(depth, rows, *refs):
    columns, weights, table_x, table_y = refs[:4]
    before = refs[4] if len(refs) > 5 else None
    out = refs[-1]
    width, length, lanes = out.shape
    half = lanes // 2
    lane = lax.broadcasted_iota(jnp.int32, (rows, lanes), 1)
    sign = jnp.where(lane < half, -1.0, 1.0)
    group = pl.program_id(0)
    sides = []
    for k in range(width):
        value = columns[pl.ds(group * width + k, rows, stride=depth), :]
        turned = pltpu.roll(value, half, 1) * sign
        sides.append(jnp.concatenate([value * weights[...], turned * weights[...]], axis=0))
    high, low = split(jnp.concatenate(sides, axis=1))
    both = dot(table_x[...], jnp.concatenate([high, low, high], axis=0))
    for k in range(width):
        value = along_lanes(both[:, k * lanes : (k + 1) * lanes], table_y[...])
        if before is not None:
            value += before[k]
        out[k] = value


def params():
    return pltpu.CompilerParams(vmem_limit_bytes=VMEM_BYTES)


def whole_spec():
    return pl.BlockSpec(memory_space=pltpu.VMEM)


def scalar_spec():
    return pl.BlockSpec(memory_space=pltpu.SMEM)


def forward(volume, halo, chunks, tables):
    depth, length, lanes = volume.shape
    steps = STEPS if halo is not None else 0
    outs = [jax.ShapeDtypeStruct((length // chunks * depth, lanes), F32)] * chunks
    specs = [whole_spec()]
    operands = [volume]
    scratch = []
    if steps:
        operands += list(halo)
        specs += [whole_spec()] * 3 + [scalar_spec()] * 2
        total = depth + 2 * steps
        padded = pltpu.VMEM((total, length + 2 * PAD, lanes), F32)
        plain = pltpu.VMEM((total, length, lanes), F32)
        scratch = [padded, padded, plain, padded, plain, plain]
    return pl.pallas_call(
        functools.partial(forward_kernel, steps, chunks, depth),
        out_shape=outs,
        in_specs=specs + [whole_spec()] * len(tables),
        out_specs=[whole_spec()] * chunks,
        scratch_shapes=scratch,
        compiler_params=params(),
        name="forward",
    )(*operands, *tables)


def middle(spectra, start, damping, matches, length_x, tables):
    slabs, submaps, rows, depth, lanes = spectra.shape
    length_z = slabs * depth
    block = pl.BlockSpec((slabs, submaps, 1, depth, lanes), lambda r: (0, 0, r, 0, 0))
    return pl.pallas_call(
        functools.partial(cross_kernel, length_x),
        out_shape=jax.ShapeDtypeStruct(spectra.shape, F32),
        grid=(rows,),
        in_specs=[scalar_spec()] * 3 + [block] + [whole_spec()] * 2,
        out_specs=block,
        scratch_shapes=[
            pltpu.VMEM((6, submaps, length_z, lanes), F32),
            pltpu.VMEM((submaps, length_z, lanes), F32),
        ],
        compiler_params=params(),
        cost_estimate=pl.CostEstimate(
            flops=6 * 2 * spectra.size * length_z * 2,
            bytes_accessed=spectra.size * 8,
            transcendentals=spectra.size,
        ),
        name="middle",
    )(start, damping, matches, spectra, *tables)


def inverse(columns, before, depth, length, tables):
    total, lanes = columns.shape
    rows = total // depth
    width = 2
    block = pl.BlockSpec((width, length, lanes), lambda g: (g, 0, 0))
    extra = [] if before is None else [before]
    return pl.pallas_call(
        functools.partial(inverse_kernel, depth, rows),
        out_shape=jax.ShapeDtypeStruct((depth, length, lanes), F32),
        grid=(depth // width,),
        in_specs=[whole_spec()] * 4 + [block] * len(extra),
        out_specs=block,
        compiler_params=params(),
        cost_estimate=pl.CostEstimate(
            flops=6 * 2 * depth * length * lanes * rows,
            bytes_accessed=columns.size * 4 + depth * length * lanes * 4 * (1 + len(extra)),
            transcendentals=0,
        ),
        name="inverse",
    )(columns, *tables, *extra)


def ends(size):
    up = [(i, i + 1) for i in range(size - 1)]
    return up, [(j, i) for i, j in up]


def diffuse_plain(field, classes, conductance):
    up, down = ends(lax.axis_size("slab"))

    def widened(volume):
        before = lax.ppermute(volume[-1:], "slab", up)
        after = lax.ppermute(volume[:1], "slab", down)
        return jnp.pad(jnp.concatenate([before, volume, after], axis=0), ((0, 0), (1, 1), (1, 1)))

    def around(volume):
        wide = widened(volume)
        core = slice(1, -1)
        for low in (slice(2, None), slice(None, -2)):
            yield wide[low, core, core]
            yield wide[core, low, core]
            yield wide[core, core, low]

    kappa = conductance[classes]
    others = list(around(kappa))
    for _ in range(STEPS):
        change = jnp.zeros_like(field)
        for near, beside in zip(around(field), others):
            change = change + 0.5 * (kappa + beside) * (near - field)
        field = field + STEP_SIZE * change
    return field


def local(occupancy, classes, conductance, damping, matches):
    slabs, pairs = lax.axis_size("slab"), lax.axis_size("pair")
    devices = slabs * pairs
    occ, cls = occupancy[0], classes[0]
    depth, length, lanes = occ.shape
    each = length // devices
    chunks = 2 if each % 2 == 0 else 1
    rows = each // chunks
    length_z = depth * slabs

    kx = np.arange(length)
    cos_x, sin_x = trig(kx, kx, length)
    take_cosine, take_sine, weights = first_column_masks(kx, length, lanes)
    table_y = right_table(half_forward(lanes))
    table_x = left_table_stack(cos_x, sin_x)
    forward_tables = (table_y, table_x, take_cosine, take_sine)
    kz = np.arange(length_z)
    cos_z, sin_z = trig(kz, kz, length_z)
    middle_tables = (left_table_stack(cos_z, sin_z), left_table(np.concatenate([cos_z, sin_z], axis=1)))
    table_back = right_table(half_inverse(lanes))

    if depth >= STEPS:
        up, down = ends(slabs)
        pack = lambda low, high: jnp.concatenate([occ[low:high], cls[low:high].astype(F32)], axis=0)
        below = lax.ppermute(pack(depth - STEPS, depth), "slab", up)
        above = lax.ppermute(pack(0, STEPS), "slab", down)
        at = lax.axis_index("slab")
        edge = jnp.stack([at > 0, at < slabs - 1]).astype(jnp.int32)
        parts = forward(occ, (cls, below, above, edge, conductance), chunks, forward_tables)
    else:
        parts = forward(diffuse_plain(occ, cls, conductance), None, chunks, forward_tables)

    me = lax.axis_index(AXES)
    straight = depth % 8 == 0
    result = None
    backs = []
    for chunk in range(chunks):
        part = parts[chunk].reshape(devices, rows, depth, lanes)
        part = lax.all_to_all(part, AXES, 0, 0, tiled=True)
        part = part.reshape(slabs, pairs, rows, depth, lanes)
        if not straight:
            part = part.transpose(1, 2, 0, 3, 4).reshape(1, pairs, rows, length_z, lanes)
        start = (chunk * (length // chunks) + me * rows).astype(jnp.int32).reshape(1)
        part = middle(part, start, damping, matches, length, middle_tables)
        if not straight:
            part = part.reshape(pairs, rows, slabs, depth, lanes).transpose(2, 0, 1, 3, 4)
        part = part.reshape(devices, rows, depth, lanes)
        backs.append(part)
    for chunk in range(chunks):
        part = lax.all_to_all(backs[chunk], AXES, 0, 0, tiled=True)
        inside = slice(chunk * (length // chunks), (chunk + 1) * (length // chunks))
        table = left_table(np.concatenate([cos_x[:, inside], sin_x[:, inside]], axis=1))
        result = inverse(
            part.reshape(-1, lanes), result, depth, length, (weights[inside], table, table_back)
        )
    return result[None]


def left_table_stack(cosine, sine):
    return np.concatenate([left_table(cosine), left_table(sine)], axis=0)


def solution(mesh):
    in_specs = (
        P(("groups", "pair"), "slab", None, None),
        P(("groups", "pair"), "slab", None, None),
        P(),
        P("groups"),
        P("groups"),
    )
    out_specs = P(("groups", "pair"), "slab", None, None)
    return jax.shard_map(local, mesh=mesh, in_specs=in_specs, out_specs=out_specs, check_vma=False)
```

```python
import functools
import math

import jax
import jax.numpy as jnp
import ml_dtypes
import numpy as np
from jax import lax
from jax.experimental import pallas as pl
from jax.experimental.pallas import tpu as pltpu
from jax.sharding import PartitionSpec as P

STEPS = 4
STEP_SIZE = 1.0 / 6.0
FLOOR_VALUE = 0.01
AXES = ("slab", "pair")
PAD = 8
BLOCK = 16
PLANES = 2
VMEM_BYTES = 60 * 1024 * 1024
BF = jnp.bfloat16
F32 = jnp.float32


def split_table(table):
    high = table.astype(ml_dtypes.bfloat16)
    low = (table - high.astype(np.float64)).astype(ml_dtypes.bfloat16)
    return high, low


def trig(rows, columns, length):
    angles = (np.asarray(rows)[:, None] * np.asarray(columns)[None, :] % length) * (2.0 * math.pi / length)
    factor = 1.0 / math.sqrt(length)
    return np.cos(angles) * factor, np.sin(angles) * factor


def left_table(table):
    high, low = split_table(table)
    return np.concatenate([high, high, low], axis=1)


def right_table(table):
    high, low = split_table(table)
    top = np.concatenate([high, low], axis=1)
    return np.concatenate([top, np.concatenate([high, np.zeros_like(low)], axis=1)], axis=0)


def half_forward(length):
    half = length // 2
    cosine, sine = trig(np.arange(length), np.arange(half + 1), length)
    return np.concatenate([cosine[:, :half], cosine[:, half:], -sine[:, 1:half]], axis=1)


def half_inverse(length):
    half = length // 2
    cosine, sine = trig(np.arange(half + 1), np.arange(length), length)
    return np.concatenate(
        [cosine[:1], 2 * cosine[1:half], cosine[half:], -2 * sine[1:half]], axis=0
    )


def first_column_masks(rows, length, lanes):
    half = lanes // 2
    lower = (rows > 0) & (rows < length // 2)
    upper = rows > length // 2
    sign = np.where(np.arange(lanes) < half, 1.0, -1.0)
    take_cosine = np.ones((rows.size, lanes))
    take_sine = np.ones((rows.size, lanes)) * sign
    take_sine[lower, 0] = 0
    take_cosine[lower, half] = 0
    take_cosine[upper, 0] = 0
    take_sine[upper, half] = 0
    weight = np.ones((rows.size, lanes))
    weight[lower, 0] = 2
    weight[lower, half] = 0
    weight[upper, 0] = 0
    weight[upper, half] = 2
    return take_cosine.astype(np.float32), take_sine.astype(np.float32), weight.astype(np.float32)


def split(values):
    high = values.astype(BF)
    return high, (values - high.astype(F32)).astype(BF)


def dot(a, b):
    return jnp.dot(a, b, preferred_element_type=F32)


def along_lanes(values, table):
    high, low = split(values)
    both = dot(jnp.concatenate([high, low], axis=1), table)
    lanes = values.shape[1]
    return both[:, :lanes] + both[:, lanes:]


def spread(first, kappa, along_x, length, lanes, total):
    zeros = jnp.zeros((PAD, lanes), F32)

    def clear(z, carry):
        for ref in (first, kappa, along_x):
            ref[z, pl.ds(0, PAD), :] = zeros
            ref[z, pl.ds(PAD + length, PAD), :] = zeros
        return carry

    lax.fori_loop(0, total, clear, 0)


def class_table(conductance, length, lanes):
    at = lax.broadcasted_iota(jnp.int32, (PAD, lanes), 1)
    entries = jnp.zeros((PAD, lanes), F32)
    for index in range(conductance.shape[0]):
        entries = jnp.where(at == index, conductance[index] * (0.5 * STEP_SIZE), entries)
    return jnp.tile(entries, (length // PAD, 1))


def face_weights(kappa, centre, along_x, along_y, along_z, total):
    length, lanes = along_y.shape[1:]
    block = BLOCK
    at = lax.broadcasted_iota(jnp.int32, (block, lanes), 1)

    def coefficients(z, carry):
        for x in range(0, length, block):
            rows = pl.ds(PAD + x, block)
            here = kappa[z, rows, :]
            x_next = kappa[z, pl.ds(PAD + x + 1, block), :]
            x_back = kappa[z, pl.ds(PAD + x - 1, block), :]
            z_next = kappa[z + 1, rows, :]
            z_back = kappa[z - 1, rows, :]
            y_next = jnp.where(at < lanes - 1, pltpu.roll(here, lanes - 1, 1), 0.0)
            y_back = jnp.where(at > 0, pltpu.roll(here, 1, 1), 0.0)
            along_x[z, rows, :] = here + x_next
            along_y[z, pl.ds(x, block), :] = jnp.where(at < lanes - 1, here + y_next, 0.0)
            along_z[z, pl.ds(x, block), :] = here + z_next
            around = (x_next + x_back) + (y_next + y_back) + (z_next + z_back)
            centre[z, pl.ds(x, block), :] = 1.0 - (6.0 * here + around)
        return carry

    lax.fori_loop(1, total - 1, coefficients, 0)
    for x in range(0, length, block):
        rows = pl.ds(PAD + x, block)
        along_z[0, pl.ds(x, block), :] = kappa[0, rows, :] + kappa[1, rows, :]


def advance_all(buffers, centre, along_x, along_y, along_z, total, steps, after_step):
    length, lanes = along_y.shape[1:]
    block = BLOCK
    old, new = buffers
    for step in range(1, steps + 1):

        def advance(group, carry):
            z0 = step + group * PLANES
            for x in range(0, length, block):
                own_rows = pl.ds(x, block)
                padded_rows = pl.ds(PAD + x, block)
                ahead = pl.ds(PAD + x + 1, block)
                back = pl.ds(PAD + x - 1, block)
                before = along_z[z0 - 1, own_rows, :] * old[z0 - 1, padded_rows, :]
                here = old[z0, padded_rows, :]
                for k in range(PLANES):
                    z = z0 + k
                    after = old[z + 1, padded_rows, :]
                    face_y = along_y[z, own_rows, :]
                    face_z = along_z[z, own_rows, :]
                    value = centre[z, own_rows, :] * here + before
                    value += face_z * after
                    value += face_y * pltpu.roll(here, lanes - 1, 1)
                    value += pltpu.roll(face_y * here, 1, 1)
                    value += along_x[z, padded_rows, :] * old[z, ahead, :]
                    value += along_x[z, back, :] * old[z, back, :]
                    new[z, padded_rows, :] = value
                    before = face_z * here
                    here = after
            return carry

        lax.fori_loop(0, (total - 2 * step) // PLANES, advance, 0)
        after_step(new)
        old, new = new, old
    return old


def inner_kernel(steps, conductance, occ, cls, out, first, second, centre, along_x, along_y, along_z, ids, sems, cls_sems):
    total, length, lanes = occ.shape
    inside = pl.ds(PAD, length)
    pieces = cls_sems.shape[0]
    size = total // pieces
    loads = []
    for k in range(pieces):
        part = pl.ds(k * size, size)
        loads.append(pltpu.make_async_copy(cls.at[part], ids.at[part], cls_sems.at[k]))
        loads[-1].start()
    field = pltpu.make_async_copy(occ, first.at[:, inside, :], sems.at[0])
    field.start()
    entries = class_table(conductance, length, lanes)
    zeros = jnp.zeros((PAD, lanes), F32)

    def clear(z, carry):
        for ref in (first, second, along_x):
            ref[z, pl.ds(0, PAD), :] = zeros
            ref[z, pl.ds(PAD + length, PAD), :] = zeros
        return carry

    lax.fori_loop(0, total, clear, 0)
    for k in range(pieces):
        loads[k].wait()

        def fill(z, carry):
            second[z, inside, :] = jnp.take_along_axis(entries, ids[z], axis=1)
            return carry

        lax.fori_loop(k * size, (k + 1) * size, fill, 0)
    face_weights(second, centre, along_x, along_y, along_z, total)
    field.wait()
    last = advance_all((first, second), centre, along_x, along_y, along_z, total, steps, lambda ref: None)
    kept = pl.ds(steps, total - 2 * steps)
    store = pltpu.make_async_copy(last.at[kept, inside, :], out.at[kept], sems.at[1])
    store.start()
    store.wait()


def outer_kernel(steps, conductance, edge, occ, cls, below, above, _, out, first, second, centre, along_x, along_y, along_z):
    total = 3 * steps
    length, lanes = occ.shape[1:]
    inside = pl.ds(PAD, length)
    side = pl.program_id(0)
    entries = class_table(conductance, length, lanes)
    spread(first, second, along_x, length, lanes, total)

    def own(z, carry):
        at = z + jnp.where(side == 0, steps, 0)
        second[at, inside, :] = jnp.take_along_axis(entries, cls[z], axis=1)
        first[at, inside, :] = occ[z]
        return carry

    lax.fori_loop(0, 2 * steps, own, 0)
    for at_side, ref, start in ((0, below, 0), (1, above, 2 * steps)):

        @pl.when((side == at_side) & (edge[at_side] > 0))
        def _():
            def halo(z, carry):
                ids = ref[steps + z].astype(jnp.int32)
                second[start + z, inside, :] = jnp.take_along_axis(entries, ids, axis=1)
                first[start + z, inside, :] = ref[z]
                return carry

            lax.fori_loop(0, steps, halo, 0)

    def clear_ghosts(ref):
        for at_side, start in ((0, 0), (1, 2 * steps)):

            @pl.when((side == at_side) & (edge[at_side] == 0))
            def _():
                def clear(z, carry):
                    ref[start + z, inside, :] = jnp.zeros((length, lanes), F32)
                    return carry

                lax.fori_loop(0, steps, clear, 0)

    clear_ghosts(first)
    clear_ghosts(second)
    face_weights(second, centre, along_x, along_y, along_z, total)
    last = advance_all((first, second), centre, along_x, along_y, along_z, total, steps, clear_ghosts)
    for k in range(steps):
        out[k] = last[steps + k, inside, :]


def spectrum_kernel(depth, volume, table_y, table_x, take_cosine, take_sine, out):
    width, length, lanes = volume.shape
    rows = take_cosine.shape[0]
    group = pl.program_id(0)
    for start in range(0, width, 2):
        sides = [along_lanes(volume[start + k], table_y[...]) for k in range(2)]
        high, low = split(jnp.concatenate(sides, axis=1))
        both = dot(table_x[...], jnp.concatenate([high, low, high], axis=0))
        for k in range(2):
            part = both[:, k * lanes : (k + 1) * lanes]
            turned = pltpu.roll(part[rows:], lanes // 2, 1)
            value = take_cosine[...] * part[:rows] + take_sine[...] * turned
            out[pl.ds(group * width + start + k, rows, stride=depth), :] = value


def cross_kernel(length_x, start, damping, matches, spectra, table_f, table_i, out, held, weight):
    slabs, submaps, _, depth, lanes = spectra.shape
    length_z = slabs * depth
    half = lanes // 2
    lane = lax.broadcasted_iota(jnp.int32, (length_z, lanes), 1)
    sign = jnp.where(lane < half, 1.0, -1.0)
    first = (lane == 0) | (lane == half)
    row = start[0] + pl.program_id(0)
    special = (row == 0) | (row == length_x // 2)
    upper = row > length_x // 2

    def signed(count, length):
        return jnp.where(count < length // 2, count, count - length).astype(F32) / length

    @pl.when(pl.program_id(0) == 0)
    def _():
        along = signed(lax.broadcasted_iota(jnp.int32, (length_z, lanes), 0), length_z)
        for s in range(submaps):
            weight[s] = jnp.exp(-damping[s] * (along * along))

    at_x = signed(row, length_x)
    lane_row = lax.broadcasted_iota(jnp.int32, (8, lanes), 1)
    count_y = jnp.where(lane_row < half, lane_row, lane_row - half)
    nyquist = ((lane_row == 0) & upper) | ((lane_row == half) & (special | upper))
    at_y = jnp.where(nyquist, -0.5, signed(count_y, lanes))
    radius = at_x * at_x + at_y * at_y

    for s in range(submaps):
        column = jnp.concatenate([spectra[i, s, 0] for i in range(slabs)], axis=0)
        high, low = split(column)
        both = dot(table_f[...], jnp.concatenate([high, low, high], axis=0))
        cosine, sine = both[:length_z], both[length_z:]
        value = cosine + sign * pltpu.roll(sine, half, 1)
        square = value * value
        held[0, s] = value
        held[1, s] = square + pltpu.roll(square, half, 1)
        held[2, s] = cosine
        held[3, s] = sine

    for s in range(submaps):
        partner = matches[s]
        own, far = held[0, s], held[0, partner]
        damp = weight[s] * jnp.tile(jnp.exp(-damping[s] * radius), (length_z // 8, 1))
        scale = damp * lax.rsqrt(held[1, s] * held[1, partner] + FLOOR_VALUE**2)
        same = own * far
        mixed = own * pltpu.roll(far, half, 1)
        real = same + pltpu.roll(same, half, 1)
        imag = mixed - pltpu.roll(mixed, half, 1)
        imag = jnp.where(lane < half, -imag, imag)
        x_here = jnp.where(lane < half, real, imag) * scale
        x_turn = jnp.where(lane < half, -imag, real) * scale
        held[4, s] = jnp.where(first & upper, x_turn, x_here)
        held[5, s] = jnp.where(first & upper, -x_here, x_turn)

        @pl.when(special)
        def _():
            own_r, own_i = held[2, s], -held[3, s]
            far_r, far_i = held[2, partner], -held[3, partner]
            size = (own_r * own_r + own_i * own_i) * (far_r * far_r + far_i * far_i)
            scale = damp * lax.rsqrt(size + FLOOR_VALUE**2)
            held[4, s] = jnp.where(first, (own_r * far_r + own_i * far_i) * scale, held[4, s])
            held[5, s] = jnp.where(first, (own_r * far_i - own_i * far_r) * scale, held[5, s])

        high, low = split(jnp.concatenate([held[4, s], held[5, s]], axis=0))
        back = dot(table_i[...], jnp.concatenate([high, low, high], axis=0))
        for i in range(slabs):
            out[i, s, 0] = back[i * depth : (i + 1) * depth]


def inverse_kernel(depth, rows, *refs):
    columns, weights, table_x, table_y = refs[:4]
    before = refs[4] if len(refs) > 5 else None
    out = refs[-1]
    width, length, lanes = out.shape
    half = lanes // 2
    lane = lax.broadcasted_iota(jnp.int32, (rows, lanes), 1)
    sign = jnp.where(lane < half, -1.0, 1.0)
    group = pl.program_id(0)
    sides = []
    for k in range(width):
        value = columns[pl.ds(group * width + k, rows, stride=depth), :]
        turned = pltpu.roll(value, half, 1) * sign
        sides.append(jnp.concatenate([value * weights[...], turned * weights[...]], axis=0))
    high, low = split(jnp.concatenate(sides, axis=1))
    both = dot(table_x[...], jnp.concatenate([high, low, high], axis=0))
    for k in range(width):
        value = along_lanes(both[:, k * lanes : (k + 1) * lanes], table_y[...])
        if before is not None:
            value += before[k]
        out[k] = value


def params():
    return pltpu.CompilerParams(vmem_limit_bytes=VMEM_BYTES)


def whole_spec():
    return pl.BlockSpec(memory_space=pltpu.VMEM)


def scalar_spec():
    return pl.BlockSpec(memory_space=pltpu.SMEM)


def any_spec():
    return pl.BlockSpec(memory_space=pl.ANY)


def diffusion_scratch(total, length, lanes):
    padded = pltpu.VMEM((total, length + 2 * PAD, lanes), F32)
    plain = pltpu.VMEM((total, length, lanes), F32)
    return [padded, padded, plain, padded, plain, plain]


def diffuse_inner(occ, cls, conductance):
    depth, length, lanes = occ.shape
    return pl.pallas_call(
        functools.partial(inner_kernel, STEPS),
        out_shape=jax.ShapeDtypeStruct(occ.shape, F32),
        in_specs=[scalar_spec(), any_spec(), any_spec()],
        out_specs=any_spec(),
        scratch_shapes=diffusion_scratch(depth, length, lanes)
        + [
            pltpu.VMEM(cls.shape, jnp.int32),
            pltpu.SemaphoreType.DMA((2,)),
            pltpu.SemaphoreType.DMA((4,)),
        ],
        compiler_params=params(),
        cost_estimate=pl.CostEstimate(
            flops=occ.size * 80, bytes_accessed=occ.size * 12, transcendentals=0
        ),
        name="inner",
    )(conductance, occ, cls)


def diffuse_outer(occ, cls, conductance, edge, below, above, inner):
    depth, length, lanes = occ.shape
    window = pl.BlockSpec((2 * STEPS, length, lanes), lambda s: (s * (depth // (2 * STEPS) - 1), 0, 0))
    kept = pl.BlockSpec((STEPS, length, lanes), lambda s: (s * (depth // STEPS - 1), 0, 0))
    return pl.pallas_call(
        functools.partial(outer_kernel, STEPS),
        out_shape=jax.ShapeDtypeStruct(occ.shape, F32),
        grid=(2,),
        in_specs=[scalar_spec(), scalar_spec(), window, window, whole_spec(), whole_spec(), any_spec()],
        out_specs=kept,
        scratch_shapes=diffusion_scratch(3 * STEPS, length, lanes),
        input_output_aliases={6: 0},
        compiler_params=params(),
        cost_estimate=pl.CostEstimate(
            flops=occ.size * 40, bytes_accessed=occ.size * 6, transcendentals=0
        ),
        name="outer",
    )(conductance, edge, occ, cls, below, above, inner)


def spectrum(volume, tables):
    depth, length, lanes = volume.shape
    table_y, table_x, take_cosine, take_sine = tables
    rows = take_cosine.shape[0]
    width = math.gcd(depth, 4)
    block = pl.BlockSpec((width, length, lanes), lambda g: (g, 0, 0))
    out = jax.ShapeDtypeStruct((rows * depth, lanes), F32)
    return pl.pallas_call(
        functools.partial(spectrum_kernel, depth),
        out_shape=out,
        grid=(depth // width,),
        in_specs=[block] + [whole_spec()] * 4,
        out_specs=pl.BlockSpec(out.shape, lambda g: (0, 0)),
        compiler_params=params(),
        cost_estimate=pl.CostEstimate(
            flops=6 * 2 * volume.size * (lanes + 2 * rows),
            bytes_accessed=volume.size * 4 + rows * depth * lanes * 4,
            transcendentals=0,
        ),
        name="spectrum",
    )(volume, table_y, table_x, take_cosine, take_sine)


def middle(spectra, start, damping, matches, length_x, tables):
    slabs, submaps, rows, depth, lanes = spectra.shape
    length_z = slabs * depth
    block = pl.BlockSpec((slabs, submaps, 1, depth, lanes), lambda r: (0, 0, r, 0, 0))
    return pl.pallas_call(
        functools.partial(cross_kernel, length_x),
        out_shape=jax.ShapeDtypeStruct(spectra.shape, F32),
        grid=(rows,),
        in_specs=[scalar_spec()] * 3 + [block] + [whole_spec()] * 2,
        out_specs=block,
        scratch_shapes=[
            pltpu.VMEM((6, submaps, length_z, lanes), F32),
            pltpu.VMEM((submaps, length_z, lanes), F32),
        ],
        compiler_params=params(),
        cost_estimate=pl.CostEstimate(
            flops=6 * 2 * spectra.size * length_z * 2,
            bytes_accessed=spectra.size * 8,
            transcendentals=spectra.size,
        ),
        name="middle",
    )(start, damping, matches, spectra, *tables)


def inverse(columns, before, depth, length, tables):
    total, lanes = columns.shape
    rows = total // depth
    width = 2
    block = pl.BlockSpec((width, length, lanes), lambda g: (g, 0, 0))
    extra = [] if before is None else [before]
    return pl.pallas_call(
        functools.partial(inverse_kernel, depth, rows),
        out_shape=jax.ShapeDtypeStruct((depth, length, lanes), F32),
        grid=(depth // width,),
        in_specs=[whole_spec()] * 4 + [block] * len(extra),
        out_specs=block,
        compiler_params=params(),
        cost_estimate=pl.CostEstimate(
            flops=6 * 2 * depth * length * lanes * rows,
            bytes_accessed=columns.size * 4 + depth * length * lanes * 4 * (1 + len(extra)),
            transcendentals=0,
        ),
        name="inverse",
    )(columns, *tables, *extra)


def ends(size):
    up = [(i, i + 1) for i in range(size - 1)]
    return up, [(j, i) for i, j in up]


def diffuse_plain(field, classes, conductance):
    up, down = ends(lax.axis_size("slab"))

    def widened(volume):
        before = lax.ppermute(volume[-1:], "slab", up)
        after = lax.ppermute(volume[:1], "slab", down)
        return jnp.pad(jnp.concatenate([before, volume, after], axis=0), ((0, 0), (1, 1), (1, 1)))

    def around(volume):
        wide = widened(volume)
        core = slice(1, -1)
        for low in (slice(2, None), slice(None, -2)):
            yield wide[low, core, core]
            yield wide[core, low, core]
            yield wide[core, core, low]

    kappa = conductance[classes]
    others = list(around(kappa))
    for _ in range(STEPS):
        change = jnp.zeros_like(field)
        for near, beside in zip(around(field), others):
            change = change + 0.5 * (kappa + beside) * (near - field)
        field = field + STEP_SIZE * change
    return field


def local(occupancy, classes, conductance, damping, matches):
    slabs, pairs = lax.axis_size("slab"), lax.axis_size("pair")
    devices = slabs * pairs
    occ, cls = occupancy[0], classes[0]
    depth, length, lanes = occ.shape
    each = length // devices
    chunks = 2 if each % 2 == 0 else 1
    rows = each // chunks
    length_z = depth * slabs

    kx = np.arange(length)
    cos_x, sin_x = trig(kx, kx, length)
    take_cosine, take_sine, weights = first_column_masks(kx, length, lanes)
    table_y = right_table(half_forward(lanes))
    kz = np.arange(length_z)
    cos_z, sin_z = trig(kz, kz, length_z)
    middle_tables = (left_table_stack(cos_z, sin_z), left_table(np.concatenate([cos_z, sin_z], axis=1)))
    table_back = right_table(half_inverse(lanes))

    if depth >= 4 * STEPS:
        up, down = ends(slabs)
        pack = lambda low, high: jnp.concatenate([occ[low:high], cls[low:high].astype(F32)], axis=0)
        below = lax.ppermute(pack(depth - STEPS, depth), "slab", up)
        above = lax.ppermute(pack(0, STEPS), "slab", down)
        at = lax.axis_index("slab")
        edge = jnp.stack([at > 0, at < slabs - 1]).astype(jnp.int32)
        inner = diffuse_inner(occ, cls, conductance)
        volume = diffuse_outer(occ, cls, conductance, edge, below, above, inner)
    else:
        volume = diffuse_plain(occ, cls, conductance)

    me = lax.axis_index(AXES)
    straight = depth % 8 == 0
    result = None
    backs = []
    for chunk in range(chunks):
        inside = slice(chunk * (length // chunks), (chunk + 1) * (length // chunks))
        table_x = left_table_stack(cos_x[inside], sin_x[inside])
        part = spectrum(volume, (table_y, table_x, take_cosine[inside], take_sine[inside]))
        part = part.reshape(devices, rows, depth, lanes)
        part = lax.all_to_all(part, AXES, 0, 0, tiled=True)
        part = part.reshape(slabs, pairs, rows, depth, lanes)
        if not straight:
            part = part.transpose(1, 2, 0, 3, 4).reshape(1, pairs, rows, length_z, lanes)
        start = (chunk * (length // chunks) + me * rows).astype(jnp.int32).reshape(1)
        part = middle(part, start, damping, matches, length, middle_tables)
        if not straight:
            part = part.reshape(pairs, rows, slabs, depth, lanes).transpose(2, 0, 1, 3, 4)
        part = part.reshape(devices, rows, depth, lanes)
        backs.append(part)
    for chunk in range(chunks):
        part = lax.all_to_all(backs[chunk], AXES, 0, 0, tiled=True)
        inside = slice(chunk * (length // chunks), (chunk + 1) * (length // chunks))
        table = left_table(np.concatenate([cos_x[:, inside], sin_x[:, inside]], axis=1))
        result = inverse(
            part.reshape(-1, lanes), result, depth, length, (weights[inside], table, table_back)
        )
    return result[None]


def left_table_stack(cosine, sine):
    return np.concatenate([left_table(cosine), left_table(sine)], axis=0)


def solution(mesh):
    in_specs = (
        P(("groups", "pair"), "slab", None, None),
        P(("groups", "pair"), "slab", None, None),
        P(),
        P("groups"),
        P("groups"),
    )
    out_specs = P(("groups", "pair"), "slab", None, None)
    return jax.shard_map(local, mesh=mesh, in_specs=in_specs, out_specs=out_specs, check_vma=False)
```

```python
import functools
import math

import jax
import jax.numpy as jnp
import ml_dtypes
import numpy as np
from jax import lax
from jax.experimental import pallas as pl
from jax.experimental.pallas import tpu as pltpu
from jax.sharding import PartitionSpec as P


STEPS = 4
STEP_SIZE = 1.0 / 6.0
FLOOR_VALUE = 0.01
AXES = ("slab", "pair")
PAD = 8
BLOCK = 16
PLANES = 2
VMEM_BYTES = 60 * 1024 * 1024
MOST_TURNS = 16
BF = jnp.bfloat16
F32 = jnp.float32


def split_table(table):
    high = table.astype(ml_dtypes.bfloat16)
    low = (table - high.astype(np.float64)).astype(ml_dtypes.bfloat16)
    return high, low


def trig(rows, columns, length):
    angles = (np.asarray(rows)[:, None] * np.asarray(columns)[None, :] % length) * (2.0 * math.pi / length)
    factor = 1.0 / math.sqrt(length)
    return np.cos(angles) * factor, np.sin(angles) * factor


def left_table(table):
    high, low = split_table(table)
    return np.concatenate([high, high, low], axis=1)


def right_table(table):
    high, low = split_table(table)
    top = np.concatenate([high, low], axis=1)
    return np.concatenate([top, np.concatenate([high, np.zeros_like(low)], axis=1)], axis=0)


def half_forward(length):
    half = length // 2
    cosine, sine = trig(np.arange(length), np.arange(half + 1), length)
    return np.concatenate([cosine[:, :half], cosine[:, half:], -sine[:, 1:half]], axis=1)


def half_inverse(length):
    half = length // 2
    cosine, sine = trig(np.arange(half + 1), np.arange(length), length)
    return np.concatenate(
        [cosine[:1], 2 * cosine[1:half], cosine[half:], -2 * sine[1:half]], axis=0
    )


def first_column_masks(rows, length, lanes):
    half = lanes // 2
    lower = (rows > 0) & (rows < length // 2)
    upper = rows > length // 2
    sign = np.where(np.arange(lanes) < half, 1.0, -1.0)
    take_cosine = np.ones((rows.size, lanes))
    take_sine = np.ones((rows.size, lanes)) * sign
    take_sine[lower, 0] = 0
    take_cosine[lower, half] = 0
    take_cosine[upper, 0] = 0
    take_sine[upper, half] = 0
    weight = np.ones((rows.size, lanes))
    weight[lower, 0] = 2
    weight[lower, half] = 0
    weight[upper, 0] = 0
    weight[upper, half] = 2
    return take_cosine.astype(np.float32), take_sine.astype(np.float32), weight.astype(np.float32)


def split(values):
    high = values.astype(BF)
    return high, (values - high.astype(F32)).astype(BF)


def dot(a, b):
    return jnp.dot(a, b, preferred_element_type=F32)


def along_lanes(values, table):
    high, low = split(values)
    both = dot(jnp.concatenate([high, low], axis=1), table)
    lanes = values.shape[1]
    return both[:, :lanes] + both[:, lanes:]


def spread(first, kappa, along_x, length, lanes, total):
    zeros = jnp.zeros((PAD, lanes), F32)

    def clear(z, carry):
        for ref in (first, kappa, along_x):
            ref[z, pl.ds(0, PAD), :] = zeros
            ref[z, pl.ds(PAD + length, PAD), :] = zeros
        return carry

    lax.fori_loop(0, total, clear, 0)


def class_table(conductance, length, lanes):
    at = lax.broadcasted_iota(jnp.int32, (PAD, lanes), 1)
    entries = jnp.zeros((PAD, lanes), F32)
    for index in range(conductance.shape[0]):
        entries = jnp.where(at == index, conductance[index] * (0.5 * STEP_SIZE), entries)
    return jnp.tile(entries, (length // PAD, 1))


def face_weights(kappa, centre, along_x, along_y, along_z, total):
    length, lanes = along_y.shape[1:]
    block = BLOCK
    at = lax.broadcasted_iota(jnp.int32, (block, lanes), 1)

    def coefficients(z, carry):
        for x in range(0, length, block):
            rows = pl.ds(PAD + x, block)
            here = kappa[z, rows, :]
            x_next = kappa[z, pl.ds(PAD + x + 1, block), :]
            x_back = kappa[z, pl.ds(PAD + x - 1, block), :]
            z_next = kappa[z + 1, rows, :]
            z_back = kappa[z - 1, rows, :]
            y_next = jnp.where(at < lanes - 1, pltpu.roll(here, lanes - 1, 1), 0.0)
            y_back = jnp.where(at > 0, pltpu.roll(here, 1, 1), 0.0)
            along_x[z, rows, :] = here + x_next
            along_y[z, pl.ds(x, block), :] = jnp.where(at < lanes - 1, here + y_next, 0.0)
            along_z[z, pl.ds(x, block), :] = here + z_next
            around = (x_next + x_back) + (y_next + y_back) + (z_next + z_back)
            centre[z, pl.ds(x, block), :] = 1.0 - (6.0 * here + around)
        return carry

    lax.fori_loop(1, total - 1, coefficients, 0)
    for x in range(0, length, block):
        rows = pl.ds(PAD + x, block)
        along_z[0, pl.ds(x, block), :] = kappa[0, rows, :] + kappa[1, rows, :]


def advance_all(buffers, centre, along_x, along_y, along_z, total, steps, after_step):
    length, lanes = along_y.shape[1:]
    block = BLOCK
    old, new = buffers
    for step in range(1, steps + 1):

        def advance(group, carry):
            z0 = step + group * PLANES
            for x in range(0, length, block):
                own_rows = pl.ds(x, block)
                padded_rows = pl.ds(PAD + x, block)
                ahead = pl.ds(PAD + x + 1, block)
                back = pl.ds(PAD + x - 1, block)
                before = along_z[z0 - 1, own_rows, :] * old[z0 - 1, padded_rows, :]
                here = old[z0, padded_rows, :]
                for k in range(PLANES):
                    z = z0 + k
                    after = old[z + 1, padded_rows, :]
                    face_y = along_y[z, own_rows, :]
                    face_z = along_z[z, own_rows, :]
                    value = centre[z, own_rows, :] * here + before
                    value += face_z * after
                    value += face_y * pltpu.roll(here, lanes - 1, 1)
                    value += pltpu.roll(face_y * here, 1, 1)
                    value += along_x[z, padded_rows, :] * old[z, ahead, :]
                    value += along_x[z, back, :] * old[z, back, :]
                    new[z, padded_rows, :] = value
                    before = face_z * here
                    here = after
            return carry

        lax.fori_loop(0, (total - 2 * step) // PLANES, advance, 0)
        after_step(new)
        old, new = new, old
    return old


def inner_kernel(steps, conductance, occ, cls, out, first, second, centre, along_x, along_y, along_z, ids, sems, cls_sems):
    total, length, lanes = occ.shape
    inside = pl.ds(PAD, length)
    pieces = cls_sems.shape[0]
    size = total // pieces
    loads = []
    for k in range(pieces):
        part = pl.ds(k * size, size)
        loads.append(pltpu.make_async_copy(cls.at[part], ids.at[part], cls_sems.at[k]))
        loads[-1].start()
    field = pltpu.make_async_copy(occ, first.at[:, inside, :], sems.at[0])
    field.start()
    entries = class_table(conductance, length, lanes)
    zeros = jnp.zeros((PAD, lanes), F32)

    def clear(z, carry):
        for ref in (first, second, along_x):
            ref[z, pl.ds(0, PAD), :] = zeros
            ref[z, pl.ds(PAD + length, PAD), :] = zeros
        return carry

    lax.fori_loop(0, total, clear, 0)
    for k in range(pieces):
        loads[k].wait()

        def fill(z, carry):
            second[z, inside, :] = jnp.take_along_axis(entries, ids[z], axis=1)
            return carry

        lax.fori_loop(k * size, (k + 1) * size, fill, 0)
    face_weights(second, centre, along_x, along_y, along_z, total)
    field.wait()
    last = advance_all((first, second), centre, along_x, along_y, along_z, total, steps, lambda ref: None)
    kept = pl.ds(steps, total - 2 * steps)
    store = pltpu.make_async_copy(last.at[kept, inside, :], out.at[kept], sems.at[1])
    store.start()
    store.wait()


def outer_kernel(steps, conductance, edge, occ, cls, below, above, _, out, first, second, centre, along_x, along_y, along_z):
    total = 3 * steps
    length, lanes = occ.shape[1:]
    inside = pl.ds(PAD, length)
    side = pl.program_id(0)
    entries = class_table(conductance, length, lanes)
    spread(first, second, along_x, length, lanes, total)

    def own(z, carry):
        at = z + jnp.where(side == 0, steps, 0)
        second[at, inside, :] = jnp.take_along_axis(entries, cls[z], axis=1)
        first[at, inside, :] = occ[z]
        return carry

    lax.fori_loop(0, 2 * steps, own, 0)
    for at_side, ref, start in ((0, below, 0), (1, above, 2 * steps)):

        @pl.when((side == at_side) & (edge[at_side] > 0))
        def _():
            def halo(z, carry):
                ids = ref[steps + z].astype(jnp.int32)
                second[start + z, inside, :] = jnp.take_along_axis(entries, ids, axis=1)
                first[start + z, inside, :] = ref[z]
                return carry

            lax.fori_loop(0, steps, halo, 0)

    def clear_ghosts(ref):
        for at_side, start in ((0, 0), (1, 2 * steps)):

            @pl.when((side == at_side) & (edge[at_side] == 0))
            def _():
                def clear(z, carry):
                    ref[start + z, inside, :] = jnp.zeros((length, lanes), F32)
                    return carry

                lax.fori_loop(0, steps, clear, 0)

    clear_ghosts(first)
    clear_ghosts(second)
    face_weights(second, centre, along_x, along_y, along_z, total)
    last = advance_all((first, second), centre, along_x, along_y, along_z, total, steps, clear_ghosts)
    for k in range(steps):
        out[k] = last[steps + k, inside, :]


def turn(me, slot, count):
    at = me + slot
    return jnp.where(at < count, at, at - count)


def spectrum_kernel(depth, me, volume, table_y, table_x, take_cosine, take_sine, *rest):
    width, _, lanes = volume.shape
    outs = rest if len(rest) == 1 else rest[:-1]
    slots = len(outs)
    rows = take_cosine.shape[0]
    group = pl.program_id(0)
    for start in range(0, width, 2):
        sides = [along_lanes(volume[start + k], table_y[...]) for k in range(2)]
        high, low = split(jnp.concatenate(sides, axis=1))
        both = dot(table_x[...], jnp.concatenate([high, low, high], axis=0))
        for k in range(2):
            part = both[:, k * lanes : (k + 1) * lanes]
            turned = pltpu.roll(part[rows:], lanes // 2, 1)
            value = take_cosine[...] * part[:rows] + take_sine[...] * turned
            z = group * width + start + k
            if slots == 1:
                outs[0][pl.ds(z, rows, stride=depth), :] = value
                continue
            held = rest[-1]
            each = rows // slots
            held[(start + k) % 2] = value
            for slot in range(slots):
                first = pl.multiple_of(turn(me[0], slot, slots) * each, each)
                outs[slot][pl.ds(z, each, stride=depth), :] = held[(start + k) % 2, pl.ds(first, each), :]


def cross_kernel(length_x, slots, start, me, damping, matches, *refs):
    sources, refs = refs[:slots], refs[slots:]
    table_f, table_i = refs[:2]
    outs, refs = refs[2 : 2 + slots], refs[2 + slots :]
    held, weight = refs[:2]
    if slots == 1:
        spectra, out = sources[0], outs[0]
        slabs, submaps, _, depth, lanes = spectra.shape
        piece = lambda i, s: spectra[i, s, 0]

        def put(i, s, value):
            out[i, s, 0] = value

    else:
        order = refs[2]
        depth, lanes = sources[0].shape[1:]
        submaps = weight.shape[0]
        slabs = slots // submaps
        for slot in range(slots):
            order[turn(me[0], (slots - slot) % slots, slots)] = sources[slot][0]
        piece = lambda i, s: order[i * submaps + s]

        def put(i, s, value):
            order[i * submaps + s] = value

    length_z = slabs * depth
    half = lanes // 2
    lane = lax.broadcasted_iota(jnp.int32, (length_z, lanes), 1)
    sign = jnp.where(lane < half, 1.0, -1.0)
    first = (lane == 0) | (lane == half)
    row = start[0] + pl.program_id(0)
    special = (row == 0) | (row == length_x // 2)
    upper = row > length_x // 2

    def signed(count, length):
        return jnp.where(count < length // 2, count, count - length).astype(F32) / length

    @pl.when(pl.program_id(0) == 0)
    def _():
        along = signed(lax.broadcasted_iota(jnp.int32, (length_z, lanes), 0), length_z)
        for s in range(submaps):
            weight[s] = jnp.exp(-damping[s] * (along * along))

    at_x = signed(row, length_x)
    lane_row = lax.broadcasted_iota(jnp.int32, (8, lanes), 1)
    count_y = jnp.where(lane_row < half, lane_row, lane_row - half)
    nyquist = ((lane_row == 0) & upper) | ((lane_row == half) & (special | upper))
    at_y = jnp.where(nyquist, -0.5, signed(count_y, lanes))
    radius = at_x * at_x + at_y * at_y

    for s in range(submaps):
        column = jnp.concatenate([piece(i, s) for i in range(slabs)], axis=0)
        high, low = split(column)
        both = dot(table_f[...], jnp.concatenate([high, low, high], axis=0))
        cosine, sine = both[:length_z], both[length_z:]
        value = cosine + sign * pltpu.roll(sine, half, 1)
        square = value * value
        held[0, s] = value
        held[1, s] = square + pltpu.roll(square, half, 1)
        held[2, s] = cosine
        held[3, s] = sine

    for s in range(submaps):
        partner = matches[s]
        own, far = held[0, s], held[0, partner]
        damp = weight[s] * jnp.tile(jnp.exp(-damping[s] * radius), (length_z // 8, 1))
        scale = damp * lax.rsqrt(held[1, s] * held[1, partner] + FLOOR_VALUE**2)
        same = own * far
        mixed = own * pltpu.roll(far, half, 1)
        real = same + pltpu.roll(same, half, 1)
        imag = mixed - pltpu.roll(mixed, half, 1)
        imag = jnp.where(lane < half, -imag, imag)
        x_here = jnp.where(lane < half, real, imag) * scale
        x_turn = jnp.where(lane < half, -imag, real) * scale
        held[4, s] = jnp.where(first & upper, x_turn, x_here)
        held[5, s] = jnp.where(first & upper, -x_here, x_turn)

        @pl.when(special)
        def _():
            own_r, own_i = held[2, s], -held[3, s]
            far_r, far_i = held[2, partner], -held[3, partner]
            size = (own_r * own_r + own_i * own_i) * (far_r * far_r + far_i * far_i)
            scale = damp * lax.rsqrt(size + FLOOR_VALUE**2)
            held[4, s] = jnp.where(first, (own_r * far_r + own_i * far_i) * scale, held[4, s])
            held[5, s] = jnp.where(first, (own_r * far_i - own_i * far_r) * scale, held[5, s])

        high, low = split(jnp.concatenate([held[4, s], held[5, s]], axis=0))
        back = dot(table_i[...], jnp.concatenate([high, low, high], axis=0))
        for i in range(slabs):
            put(i, s, back[i * depth : (i + 1) * depth])

    if slots > 1:
        for slot in range(slots):
            outs[slot][0] = order[turn(me[0], slot, slots)]


def inverse_kernel(depth, rows, slots, added, me, *refs):
    columns, refs = refs[:slots], refs[slots:]
    weights, table_x, table_y = refs[:3]
    before = refs[3] if added else None
    out = refs[3 + added]
    each = rows // slots
    width, _, lanes = out.shape
    half = lanes // 2
    lane = lax.broadcasted_iota(jnp.int32, (rows, lanes), 1)
    sign = jnp.where(lane < half, -1.0, 1.0)
    group = pl.program_id(0)
    sides = []
    for k in range(width):
        z = group * width + k
        if slots == 1:
            value = columns[0][pl.ds(z, rows, stride=depth), :]
        else:
            held = refs[-1]
            for slot in range(slots):
                first = pl.multiple_of(turn(me[0], (slots - slot) % slots, slots) * each, each)
                held[k, pl.ds(first, each), :] = columns[slot][pl.ds(z, each, stride=depth), :]
            value = held[k]
        turned = pltpu.roll(value, half, 1) * sign
        sides.append(jnp.concatenate([value * weights[...], turned * weights[...]], axis=0))
    high, low = split(jnp.concatenate(sides, axis=1))
    both = dot(table_x[...], jnp.concatenate([high, low, high], axis=0))
    for k in range(width):
        value = along_lanes(both[:, k * lanes : (k + 1) * lanes], table_y[...])
        if before is not None:
            value += before[k]
        out[k] = value


def params():
    return pltpu.CompilerParams(vmem_limit_bytes=VMEM_BYTES)


def whole_spec():
    return pl.BlockSpec(memory_space=pltpu.VMEM)


def scalar_spec():
    return pl.BlockSpec(memory_space=pltpu.SMEM)


def any_spec():
    return pl.BlockSpec(memory_space=pl.ANY)


def diffusion_scratch(total, length, lanes):
    padded = pltpu.VMEM((total, length + 2 * PAD, lanes), F32)
    plain = pltpu.VMEM((total, length, lanes), F32)
    return [padded, padded, plain, padded, plain, plain]


def diffuse_inner(occ, cls, conductance):
    depth, length, lanes = occ.shape
    return pl.pallas_call(
        functools.partial(inner_kernel, STEPS),
        out_shape=jax.ShapeDtypeStruct(occ.shape, F32),
        in_specs=[scalar_spec(), any_spec(), any_spec()],
        out_specs=any_spec(),
        scratch_shapes=diffusion_scratch(depth, length, lanes)
        + [
            pltpu.VMEM(cls.shape, jnp.int32),
            pltpu.SemaphoreType.DMA((2,)),
            pltpu.SemaphoreType.DMA((4,)),
        ],
        compiler_params=params(),
        cost_estimate=pl.CostEstimate(
            flops=occ.size * 80, bytes_accessed=occ.size * 12, transcendentals=0
        ),
        name="inner",
    )(conductance, occ, cls)


def diffuse_outer(occ, cls, conductance, edge, below, above, inner):
    depth, length, lanes = occ.shape
    window = pl.BlockSpec((2 * STEPS, length, lanes), lambda s: (s * (depth // (2 * STEPS) - 1), 0, 0))
    kept = pl.BlockSpec((STEPS, length, lanes), lambda s: (s * (depth // STEPS - 1), 0, 0))
    return pl.pallas_call(
        functools.partial(outer_kernel, STEPS),
        out_shape=jax.ShapeDtypeStruct(occ.shape, F32),
        grid=(2,),
        in_specs=[scalar_spec(), scalar_spec(), window, window, whole_spec(), whole_spec(), any_spec()],
        out_specs=kept,
        scratch_shapes=diffusion_scratch(3 * STEPS, length, lanes),
        input_output_aliases={6: 0},
        compiler_params=params(),
        cost_estimate=pl.CostEstimate(
            flops=occ.size * 40, bytes_accessed=occ.size * 6, transcendentals=0
        ),
        name="outer",
    )(conductance, edge, occ, cls, below, above, inner)


def spectrum(volume, me, slots, tables):
    depth, length, lanes = volume.shape
    table_y, table_x, take_cosine, take_sine = tables
    rows = take_cosine.shape[0]
    width = math.gcd(depth, 4)
    block = pl.BlockSpec((width, length, lanes), lambda g: (g, 0, 0))
    out = jax.ShapeDtypeStruct((rows // slots * depth, lanes), F32)
    return pl.pallas_call(
        functools.partial(spectrum_kernel, depth),
        out_shape=[out] * slots,
        grid=(depth // width,),
        in_specs=[scalar_spec(), block] + [whole_spec()] * 4,
        out_specs=[pl.BlockSpec(out.shape, lambda g: (0, 0))] * slots,
        scratch_shapes=[pltpu.VMEM((2, rows, lanes), F32)] if slots > 1 else [],
        compiler_params=params(),
        cost_estimate=pl.CostEstimate(
            flops=6 * 2 * volume.size * (lanes + 2 * rows),
            bytes_accessed=volume.size * 4 + rows * depth * lanes * 4,
            transcendentals=0,
        ),
        name="spectrum",
    )(me, volume, table_y, table_x, take_cosine, take_sine)


def middle(sources, dims, start, me, damping, matches, length_x, tables):
    slabs, submaps, rows, depth, lanes = dims
    length_z = slabs * depth
    slots = len(sources)
    size = math.prod(dims)
    scratch = [
        pltpu.VMEM((6, submaps, length_z, lanes), F32),
        pltpu.VMEM((submaps, length_z, lanes), F32),
    ]
    if slots == 1:
        block = pl.BlockSpec((slabs, submaps, 1, depth, lanes), lambda r: (0, 0, r, 0, 0))
    else:
        block = pl.BlockSpec((1, depth, lanes), lambda r: (r, 0, 0))
        scratch.append(pltpu.VMEM((slots, depth, lanes), F32))
    return pl.pallas_call(
        functools.partial(cross_kernel, length_x, slots),
        out_shape=[jax.ShapeDtypeStruct(part.shape, F32) for part in sources],
        grid=(rows,),
        in_specs=[scalar_spec()] * 4 + [block] * slots + [whole_spec()] * 2,
        out_specs=[block] * slots,
        scratch_shapes=scratch,
        compiler_params=params(),
        cost_estimate=pl.CostEstimate(
            flops=6 * 2 * size * length_z * 2, bytes_accessed=size * 8, transcendentals=size
        ),
        name="middle",
    )(start, me, damping, matches, *sources, *tables)


def inverse(columns, me, before, depth, length, tables):
    slots = len(columns)
    lanes = columns[0].shape[1]
    rows = slots * columns[0].shape[0] // depth
    width = 2
    block = pl.BlockSpec((width, length, lanes), lambda g: (g, 0, 0))
    extra = [] if before is None else [before]
    return pl.pallas_call(
        functools.partial(inverse_kernel, depth, rows, slots, len(extra)),
        out_shape=jax.ShapeDtypeStruct((depth, length, lanes), F32),
        grid=(depth // width,),
        in_specs=[scalar_spec()] + [whole_spec()] * (slots + 3) + [block] * len(extra),
        out_specs=block,
        scratch_shapes=[pltpu.VMEM((width, rows, lanes), F32)] if slots > 1 else [],
        compiler_params=params(),
        cost_estimate=pl.CostEstimate(
            flops=6 * 2 * depth * length * lanes * rows,
            bytes_accessed=rows * depth * lanes * 4 + depth * length * lanes * 4 * (1 + len(extra)),
            transcendentals=0,
        ),
        name="inverse",
    )(me, *columns, *tables, *extra)


def ends(size):
    up = [(i, i + 1) for i in range(size - 1)]
    return up, [(j, i) for i, j in up]


def diffuse_plain(field, classes, conductance):
    up, down = ends(lax.axis_size("slab"))

    def widened(volume):
        before = lax.ppermute(volume[-1:], "slab", up)
        after = lax.ppermute(volume[:1], "slab", down)
        return jnp.pad(jnp.concatenate([before, volume, after], axis=0), ((0, 0), (1, 1), (1, 1)))

    def around(volume):
        wide = widened(volume)
        core = slice(1, -1)
        for low in (slice(2, None), slice(None, -2)):
            yield wide[low, core, core]
            yield wide[core, low, core]
            yield wide[core, core, low]

    kappa = conductance[classes]
    others = list(around(kappa))
    for _ in range(STEPS):
        change = jnp.zeros_like(field)
        for near, beside in zip(around(field), others):
            change = change + 0.5 * (kappa + beside) * (near - field)
        field = field + STEP_SIZE * change
    return field


def local(occupancy, classes, conductance, damping, matches):
    slabs, pairs = lax.axis_size("slab"), lax.axis_size("pair")
    devices = slabs * pairs
    occ, cls = occupancy[0], classes[0]
    depth, length, lanes = occ.shape
    each = length // devices
    chunks = 2 if each % 2 == 0 else 1
    rows = each // chunks
    length_z = depth * slabs

    kx = np.arange(length)
    cos_x, sin_x = trig(kx, kx, length)
    take_cosine, take_sine, weights = first_column_masks(kx, length, lanes)
    table_y = right_table(half_forward(lanes))
    kz = np.arange(length_z)
    cos_z, sin_z = trig(kz, kz, length_z)
    middle_tables = (left_table_stack(cos_z, sin_z), left_table(np.concatenate([cos_z, sin_z], axis=1)))
    table_back = right_table(half_inverse(lanes))

    if depth >= 4 * STEPS:
        up, down = ends(slabs)
        pack = lambda low, high: jnp.concatenate([occ[low:high], cls[low:high].astype(F32)], axis=0)
        below = lax.ppermute(pack(depth - STEPS, depth), "slab", up)
        above = lax.ppermute(pack(0, STEPS), "slab", down)
        at = lax.axis_index("slab")
        edge = jnp.stack([at > 0, at < slabs - 1]).astype(jnp.int32)
        inner = diffuse_inner(occ, cls, conductance)
        volume = diffuse_outer(occ, cls, conductance, edge, below, above, inner)
    else:
        volume = diffuse_plain(occ, cls, conductance)

    me = lax.axis_index(AXES).astype(jnp.int32).reshape(1)
    straight = depth % 8 == 0
    span = length // chunks

    def turns(chunk):
        return chunk % 2 == 1 and rows % 8 == 0 and devices <= MOST_TURNS

    def exchange(parts):
        if len(parts) == 1:
            part = parts[0].reshape(devices, rows, depth, lanes)
            return [lax.all_to_all(part, AXES, 0, 0, tiled=True)]
        moved = [parts[0]]
        for slot in range(1, devices):
            pairs_of = [(i, (i + slot) % devices) for i in range(devices)]
            moved.append(lax.ppermute(parts[slot], AXES, pairs_of))
        return moved

    dims = (slabs, pairs, rows, depth, lanes)
    backs = []
    for chunk in range(chunks):
        inside = slice(chunk * span, (chunk + 1) * span)
        table_x = left_table_stack(cos_x[inside], sin_x[inside])
        slots = devices if turns(chunk) else 1
        parts = spectrum(
            volume, me, slots, (table_y, table_x, take_cosine[inside], take_sine[inside])
        )
        parts = exchange(parts)
        start = chunk * span + me * rows
        if slots > 1:
            parts = [part.reshape(rows, depth, lanes) for part in parts]
            parts = middle(parts, dims, start, me, damping, matches, length, middle_tables)
            backs.append([part.reshape(rows * depth, lanes) for part in parts])
            continue
        part = parts[0].reshape(dims)
        shape = dims
        if not straight:
            shape = (1, pairs, rows, length_z, lanes)
            part = part.transpose(1, 2, 0, 3, 4).reshape(shape)
        part = middle([part], shape, start, me, damping, matches, length, middle_tables)[0]
        if not straight:
            part = part.reshape(pairs, rows, slabs, depth, lanes).transpose(2, 0, 1, 3, 4)
        backs.append([part])
    result = None
    for chunk in range(chunks):
        parts = [part.reshape(-1, lanes) for part in exchange(backs[chunk])]
        inside = slice(chunk * span, (chunk + 1) * span)
        table = left_table(np.concatenate([cos_x[:, inside], sin_x[:, inside]], axis=1))
        result = inverse(parts, me, result, depth, length, (weights[inside], table, table_back))
    return result[None]


def left_table_stack(cosine, sine):
    return np.concatenate([left_table(cosine), left_table(sine)], axis=0)


def solution(mesh):
    in_specs = (
        P(("groups", "pair"), "slab", None, None),
        P(("groups", "pair"), "slab", None, None),
        P(),
        P("groups"),
        P("groups"),
    )
    out_specs = P(("groups", "pair"), "slab", None, None)

    return jax.shard_map(local, mesh=mesh, in_specs=in_specs, out_specs=out_specs, check_vma=False)
```

```python
import functools
import math

import jax
import jax.numpy as jnp
import ml_dtypes
import numpy as np
from jax import lax
from jax.experimental import pallas as pl
from jax.experimental.pallas import tpu as pltpu
from jax.sharding import PartitionSpec as P


STEPS = 4
STEP_SIZE = 1.0 / 6.0
FLOOR_VALUE = 0.01
AXES = ("slab", "pair")
PAD = 8
BLOCK = 16
WIDTH = 8
PLANES = 2
VMEM_BYTES = 60 * 1024 * 1024
MOST_TURNS = 16
BF = jnp.bfloat16
F32 = jnp.float32


def split_table(table):
    high = table.astype(ml_dtypes.bfloat16)
    low = (table - high.astype(np.float64)).astype(ml_dtypes.bfloat16)
    return high, low


def trig(rows, columns, length):
    angles = (np.asarray(rows)[:, None] * np.asarray(columns)[None, :] % length) * (2.0 * math.pi / length)
    factor = 1.0 / math.sqrt(length)
    return np.cos(angles) * factor, np.sin(angles) * factor


def left_table(table):
    return np.concatenate(split_table(table), axis=1)


def widen(table, wide):
    depth = table.shape[1] // 2
    wide[:, :depth] = table[:, :depth]
    wide[:, depth:] = table[...]


def wide_scratch(table):
    return pltpu.VMEM((table.shape[0], table.shape[1] * 3 // 2), BF)


def right_table(table):
    high, low = split_table(table)
    top = np.concatenate([high, low], axis=1)
    return np.concatenate([top, np.concatenate([high, np.zeros_like(low)], axis=1)], axis=0)


def half_forward(length):
    half = length // 2
    cosine, sine = trig(np.arange(length), np.arange(half + 1), length)
    return np.concatenate([cosine[:, :half], cosine[:, half:], -sine[:, 1:half]], axis=1)


def half_inverse(length):
    half = length // 2
    cosine, sine = trig(np.arange(half + 1), np.arange(length), length)
    return np.concatenate(
        [cosine[:1], 2 * cosine[1:half], cosine[half:], -2 * sine[1:half]], axis=0
    )


def first_column_masks(rows, length, lanes):
    half = lanes // 2
    lower = (rows > 0) & (rows < length // 2)
    upper = rows > length // 2
    sign = np.where(np.arange(lanes) < half, 1.0, -1.0)
    take_cosine = np.ones((rows.size, lanes))
    take_sine = np.ones((rows.size, lanes)) * sign
    take_sine[lower, 0] = 0
    take_cosine[lower, half] = 0
    take_cosine[upper, 0] = 0
    take_sine[upper, half] = 0
    weight = np.ones((rows.size, lanes))
    weight[lower, 0] = 2
    weight[lower, half] = 0
    weight[upper, 0] = 0
    weight[upper, half] = 2
    return take_cosine.astype(np.float32), take_sine.astype(np.float32), weight.astype(np.float32)


def split(values):
    high = values.astype(BF)
    return high, (values - high.astype(F32)).astype(BF)


def dot(a, b):
    return jnp.dot(a, b, preferred_element_type=F32)


def along_lanes(values, table):
    high, low = split(values)
    both = dot(jnp.concatenate([high, low], axis=1), table)
    lanes = values.shape[1]
    return both[:, :lanes] + both[:, lanes:]


def spread(first, kappa, along_x, length, lanes, total):
    zeros = jnp.zeros((PAD, lanes), F32)

    def clear(z, carry):
        for ref in (first, kappa, along_x):
            ref[z, pl.ds(0, PAD), :] = zeros
            ref[z, pl.ds(PAD + length, PAD), :] = zeros
        return carry

    lax.fori_loop(0, total, clear, 0)


def class_table(conductance, length, lanes):
    at = lax.broadcasted_iota(jnp.int32, (PAD, lanes), 1)
    entries = jnp.zeros((PAD, lanes), F32)
    for index in range(conductance.shape[0]):
        entries = jnp.where(at == index, conductance[index] * (0.5 * STEP_SIZE), entries)
    return jnp.tile(entries, (length // PAD, 1))


def face_weights(kappa, centre, along_x, along_y, along_z, total):
    length, lanes = along_y.shape[1:]
    block = BLOCK
    at = lax.broadcasted_iota(jnp.int32, (block, lanes), 1)

    def coefficients(z, carry):
        for x in range(0, length, block):
            rows = pl.ds(PAD + x, block)
            here = kappa[z, rows, :]
            x_next = kappa[z, pl.ds(PAD + x + 1, block), :]
            x_back = kappa[z, pl.ds(PAD + x - 1, block), :]
            z_next = kappa[z + 1, rows, :]
            z_back = kappa[z - 1, rows, :]
            y_next = jnp.where(at < lanes - 1, pltpu.roll(here, lanes - 1, 1), 0.0)
            y_back = jnp.where(at > 0, pltpu.roll(here, 1, 1), 0.0)
            along_x[z, rows, :] = here + x_next
            along_y[z, pl.ds(x, block), :] = jnp.where(at < lanes - 1, here + y_next, 0.0)
            along_z[z, pl.ds(x, block), :] = here + z_next
            around = (x_next + x_back) + (y_next + y_back) + (z_next + z_back)
            centre[z, pl.ds(x, block), :] = 1.0 - (6.0 * here + around)
        return carry

    lax.fori_loop(1, total - 1, coefficients, 0)
    for x in range(0, length, block):
        rows = pl.ds(PAD + x, block)
        along_z[0, pl.ds(x, block), :] = kappa[0, rows, :] + kappa[1, rows, :]


def advance_all(buffers, centre, along_x, along_y, along_z, total, steps, after_step):
    length, lanes = along_y.shape[1:]
    block = BLOCK
    old, new = buffers
    for step in range(1, steps + 1):

        def advance(group, carry):
            z0 = step + group * PLANES
            for x in range(0, length, block):
                own_rows = pl.ds(x, block)
                padded_rows = pl.ds(PAD + x, block)
                ahead = pl.ds(PAD + x + 1, block)
                back = pl.ds(PAD + x - 1, block)
                before = along_z[z0 - 1, own_rows, :] * old[z0 - 1, padded_rows, :]
                here = old[z0, padded_rows, :]
                for k in range(PLANES):
                    z = z0 + k
                    after = old[z + 1, padded_rows, :]
                    face_y = along_y[z, own_rows, :]
                    face_z = along_z[z, own_rows, :]
                    value = centre[z, own_rows, :] * here + before
                    value += face_z * after
                    value += face_y * pltpu.roll(here, lanes - 1, 1)
                    value += pltpu.roll(face_y * here, 1, 1)
                    value += along_x[z, padded_rows, :] * old[z, ahead, :]
                    value += along_x[z, back, :] * old[z, back, :]
                    new[z, padded_rows, :] = value
                    before = face_z * here
                    here = after
            return carry

        lax.fori_loop(0, (total - 2 * step) // PLANES, advance, 0)
        after_step(new)
        old, new = new, old
    return old


def inner_kernel(steps, conductance, occ, cls, out, first, second, centre, along_x, along_y, along_z, ids, sems, cls_sems):
    total, length, lanes = occ.shape
    inside = pl.ds(PAD, length)
    pieces = cls_sems.shape[0]
    size = total // pieces
    loads = []
    for k in range(pieces):
        part = pl.ds(k * size, size)
        loads.append(pltpu.make_async_copy(cls.at[part], ids.at[part], cls_sems.at[k]))
        loads[-1].start()
    field = pltpu.make_async_copy(occ, first.at[:, inside, :], sems.at[0])
    field.start()
    entries = class_table(conductance, length, lanes)
    zeros = jnp.zeros((PAD, lanes), F32)

    def clear(z, carry):
        for ref in (first, second, along_x):
            ref[z, pl.ds(0, PAD), :] = zeros
            ref[z, pl.ds(PAD + length, PAD), :] = zeros
        return carry

    lax.fori_loop(0, total, clear, 0)
    for k in range(pieces):
        loads[k].wait()

        def fill(z, carry):
            second[z, inside, :] = jnp.take_along_axis(entries, ids[z], axis=1)
            return carry

        lax.fori_loop(k * size, (k + 1) * size, fill, 0)
    face_weights(second, centre, along_x, along_y, along_z, total)
    field.wait()
    last = advance_all((first, second), centre, along_x, along_y, along_z, total, steps, lambda ref: None)
    kept = pl.ds(steps, total - 2 * steps)
    store = pltpu.make_async_copy(last.at[kept, inside, :], out.at[kept], sems.at[1])
    store.start()
    store.wait()


def outer_kernel(steps, conductance, edge, occ, cls, below, above, _, out, first, second, centre, along_x, along_y, along_z):
    total = 3 * steps
    length, lanes = occ.shape[1:]
    inside = pl.ds(PAD, length)
    side = pl.program_id(0)
    entries = class_table(conductance, length, lanes)
    spread(first, second, along_x, length, lanes, total)

    def own(z, carry):
        at = z + jnp.where(side == 0, steps, 0)
        second[at, inside, :] = jnp.take_along_axis(entries, cls[z], axis=1)
        first[at, inside, :] = occ[z]
        return carry

    lax.fori_loop(0, 2 * steps, own, 0)
    for at_side, ref, start in ((0, below, 0), (1, above, 2 * steps)):

        @pl.when((side == at_side) & (edge[at_side] > 0))
        def _():
            def halo(z, carry):
                ids = ref[steps + z].astype(jnp.int32)
                second[start + z, inside, :] = jnp.take_along_axis(entries, ids, axis=1)
                first[start + z, inside, :] = ref[z]
                return carry

            lax.fori_loop(0, steps, halo, 0)

    def clear_ghosts(ref):
        for at_side, start in ((0, 0), (1, 2 * steps)):

            @pl.when((side == at_side) & (edge[at_side] == 0))
            def _():
                def clear(z, carry):
                    ref[start + z, inside, :] = jnp.zeros((length, lanes), F32)
                    return carry

                lax.fori_loop(0, steps, clear, 0)

    clear_ghosts(first)
    clear_ghosts(second)
    face_weights(second, centre, along_x, along_y, along_z, total)
    last = advance_all((first, second), centre, along_x, along_y, along_z, total, steps, clear_ghosts)
    for k in range(steps):
        out[k] = last[steps + k, inside, :]


def turn(me, slot, count):
    at = me + slot
    return jnp.where(at < count, at, at - count)


def spectrum_kernel(me, volume, table_y, table_x, take_cosine, take_sine, *rest):
    wide, outs = rest[-1], rest[:-1] if len(rest) == 2 else rest[:-2]
    width, _, lanes = volume.shape
    slots = len(outs)
    rows = take_cosine.shape[0]

    @pl.when(pl.program_id(0) == 0)
    def _():
        widen(table_x, wide)

    for start in range(0, width, 2):
        sides = [along_lanes(volume[start + k], table_y[...]) for k in range(2)]
        high, low = split(jnp.concatenate(sides, axis=1))
        both = dot(wide[...], jnp.concatenate([high, low, high], axis=0))
        for k in range(2):
            part = both[:, k * lanes : (k + 1) * lanes]
            turned = pltpu.roll(part[rows:], lanes // 2, 1)
            value = take_cosine[...] * part[:rows] + take_sine[...] * turned
            if slots == 1:
                devices, _, each, _ = outs[0].shape
                outs[0][:, start + k] = value.reshape(devices, each, lanes)
                continue
            held = rest[-2]
            each = rows // slots
            held[k] = value.reshape(slots, each, lanes)
            for slot in range(slots):
                outs[slot][start + k] = held[k, turn(me[0], slot, slots)]


def cross_kernel(length_x, dims, start, me, damping, matches, *refs):
    slabs, submaps, rows, depth, lanes = dims
    slots = (len(refs) - 6) // 2 if len(refs) > 8 else 1
    sources, (table_f, table_i) = refs[:slots], refs[slots : slots + 2]
    outs, (held, weight, wide_f, wide_i) = refs[slots + 2 : 2 * slots + 2], refs[2 * slots + 2 : 2 * slots + 6]
    each = depth * rows
    source, out = (sources[0], outs[0]) if slots == 1 else (refs[-1], refs[-1])
    length_z = slabs * depth
    half = lanes // 2
    lane = lax.broadcasted_iota(jnp.int32, (length_z, lanes), 1)
    sign = jnp.where(lane < half, 1.0, -1.0)
    first = (lane == 0) | (lane == half)

    def signed(count, length):
        return jnp.where(count < length // 2, count, count - length).astype(F32) / length

    widen(table_f, wide_f)
    widen(table_i, wide_i)
    along = signed(lax.broadcasted_iota(jnp.int32, (length_z, lanes), 0), length_z)
    for s in range(submaps):
        weight[s] = jnp.exp(-damping[s] * (along * along))
    if slots > 1:
        for slot in range(slots):
            at = turn(me[0], (slots - slot) % slots, slots)
            source[pl.ds(pl.multiple_of(at * each, each), each), :] = sources[slot][...]

    def one_row(r, carry):
        row = start[0] + r
        special = (row == 0) | (row == length_x // 2)
        upper = row > length_x // 2
        at_x = signed(row, length_x)
        lane_row = lax.broadcasted_iota(jnp.int32, (8, lanes), 1)
        count_y = jnp.where(lane_row < half, lane_row, lane_row - half)
        nyquist = ((lane_row == 0) & upper) | ((lane_row == half) & (special | upper))
        at_y = jnp.where(nyquist, -0.5, signed(count_y, lanes))
        radius = at_x * at_x + at_y * at_y

        for s in range(submaps):
            parts = [
                source[pl.ds((i * submaps + s) * each + r, depth, stride=rows), :] for i in range(slabs)
            ]
            column = parts[0] if slabs == 1 else jnp.concatenate(parts, axis=0)
            high, low = split(column)
            both = dot(wide_f[...], jnp.concatenate([high, low, high], axis=0))
            cosine, sine = both[:length_z], both[length_z:]
            value = cosine + sign * pltpu.roll(sine, half, 1)
            square = value * value
            held[0, s] = value
            held[1, s] = square + pltpu.roll(square, half, 1)
            held[2, s] = cosine
            held[3, s] = sine

        for s in range(submaps):
            partner = matches[s]
            own, far = held[0, s], held[0, partner]
            damp = weight[s] * jnp.tile(jnp.exp(-damping[s] * radius), (length_z // 8, 1))
            scale = damp * lax.rsqrt(held[1, s] * held[1, partner] + FLOOR_VALUE**2)
            same = own * far
            mixed = own * pltpu.roll(far, half, 1)
            real = same + pltpu.roll(same, half, 1)
            imag = mixed - pltpu.roll(mixed, half, 1)
            imag = jnp.where(lane < half, -imag, imag)
            x_here = jnp.where(lane < half, real, imag) * scale
            x_turn = jnp.where(lane < half, -imag, real) * scale
            held[4, s] = jnp.where(first & upper, x_turn, x_here)
            held[5, s] = jnp.where(first & upper, -x_here, x_turn)

            @pl.when(special)
            def _():
                own_r, own_i = held[2, s], -held[3, s]
                far_r, far_i = held[2, partner], -held[3, partner]
                size = (own_r * own_r + own_i * own_i) * (far_r * far_r + far_i * far_i)
                scale = damp * lax.rsqrt(size + FLOOR_VALUE**2)
                held[4, s] = jnp.where(first, (own_r * far_r + own_i * far_i) * scale, held[4, s])
                held[5, s] = jnp.where(first, (own_r * far_i - own_i * far_r) * scale, held[5, s])

            high, low = split(jnp.concatenate([held[4, s], held[5, s]], axis=0))
            back = dot(wide_i[...], jnp.concatenate([high, low, high], axis=0))
            for i in range(slabs):
                place = pl.ds((i * submaps + s) * each + r, depth, stride=rows)
                out[place, :] = back[i * depth : (i + 1) * depth]
        return carry

    lax.fori_loop(0, rows, one_row, 0)
    if slots > 1:
        for slot in range(slots):
            at = turn(me[0], slot, slots)
            outs[slot][...] = out[pl.ds(pl.multiple_of(at * each, each), each), :]


def inverse_kernel(rows, slots, added, me, *refs):
    columns, refs = refs[:slots], refs[slots:]
    weights, table_x, table_y = refs[:3]
    before = refs[3] if added else None
    out, wide = refs[3 + added], refs[4 + added]

    @pl.when(pl.program_id(0) == 0)
    def _():
        widen(table_x, wide)

    width, _, lanes = out.shape
    half = lanes // 2
    lane = lax.broadcasted_iota(jnp.int32, (rows, lanes), 1)
    sign = jnp.where(lane < half, -1.0, 1.0)
    for start in range(0, width, 2):
        sides = []
        for k in range(2):
            if slots == 1:
                value = columns[0][:, start + k].reshape(rows, lanes)
            else:
                held = refs[-1]
                for slot in range(slots):
                    held[k, turn(me[0], (slots - slot) % slots, slots)] = columns[slot][start + k]
                value = held[k].reshape(rows, lanes)
            turned = pltpu.roll(value, half, 1) * sign
            sides.append(jnp.concatenate([value * weights[...], turned * weights[...]], axis=0))
        high, low = split(jnp.concatenate(sides, axis=1))
        both = dot(wide[...], jnp.concatenate([high, low, high], axis=0))
        for k in range(2):
            value = along_lanes(both[:, k * lanes : (k + 1) * lanes], table_y[...])
            if before is not None:
                value += before[start + k]
            out[start + k] = value


def params():
    return pltpu.CompilerParams(vmem_limit_bytes=VMEM_BYTES)


def whole_spec():
    return pl.BlockSpec(memory_space=pltpu.VMEM)


def scalar_spec():
    return pl.BlockSpec(memory_space=pltpu.SMEM)


def any_spec():
    return pl.BlockSpec(memory_space=pl.ANY)


def diffusion_scratch(total, length, lanes):
    padded = pltpu.VMEM((total, length + 2 * PAD, lanes), F32)
    plain = pltpu.VMEM((total, length, lanes), F32)
    return [padded, padded, plain, padded, plain, plain]


def diffuse_inner(occ, cls, conductance):
    depth, length, lanes = occ.shape
    return pl.pallas_call(
        functools.partial(inner_kernel, STEPS),
        out_shape=jax.ShapeDtypeStruct(occ.shape, F32),
        in_specs=[scalar_spec(), any_spec(), any_spec()],
        out_specs=any_spec(),
        scratch_shapes=diffusion_scratch(depth, length, lanes)
        + [
            pltpu.VMEM(cls.shape, jnp.int32),
            pltpu.SemaphoreType.DMA((2,)),
            pltpu.SemaphoreType.DMA((4,)),
        ],
        compiler_params=params(),
        cost_estimate=pl.CostEstimate(
            flops=occ.size * 80, bytes_accessed=occ.size * 12, transcendentals=0
        ),
        name="inner",
    )(conductance, occ, cls)


def diffuse_outer(occ, cls, conductance, edge, below, above, inner):
    depth, length, lanes = occ.shape
    window = pl.BlockSpec((2 * STEPS, length, lanes), lambda s: (s * (depth // (2 * STEPS) - 1), 0, 0))
    kept = pl.BlockSpec((STEPS, length, lanes), lambda s: (s * (depth // STEPS - 1), 0, 0))
    return pl.pallas_call(
        functools.partial(outer_kernel, STEPS),
        out_shape=jax.ShapeDtypeStruct(occ.shape, F32),
        grid=(2,),
        in_specs=[scalar_spec(), scalar_spec(), window, window, whole_spec(), whole_spec(), any_spec()],
        out_specs=kept,
        scratch_shapes=diffusion_scratch(3 * STEPS, length, lanes),
        input_output_aliases={6: 0},
        compiler_params=params(),
        cost_estimate=pl.CostEstimate(
            flops=occ.size * 40, bytes_accessed=occ.size * 6, transcendentals=0
        ),
        name="outer",
    )(conductance, edge, occ, cls, below, above, inner)


def spectrum(volume, me, devices, slots, tables):
    depth, length, lanes = volume.shape
    table_y, table_x, take_cosine, take_sine = tables
    rows = take_cosine.shape[0]
    each = rows // devices
    width = math.gcd(depth, WIDTH)
    block = pl.BlockSpec((width, length, lanes), lambda g: (g, 0, 0))
    if slots == 1:
        out = jax.ShapeDtypeStruct((devices, depth, each, lanes), F32)
        kept = pl.BlockSpec((devices, width, each, lanes), lambda g: (0, g, 0, 0))
    else:
        out = jax.ShapeDtypeStruct((depth, each, lanes), F32)
        kept = pl.BlockSpec((width, each, lanes), lambda g: (g, 0, 0))
    return pl.pallas_call(
        spectrum_kernel,
        out_shape=[out] * slots,
        grid=(depth // width,),
        in_specs=[scalar_spec(), block] + [whole_spec()] * 4,
        out_specs=[kept] * slots,
        scratch_shapes=([pltpu.VMEM((2, slots, each, lanes), F32)] if slots > 1 else [])
        + [wide_scratch(table_x)],
        compiler_params=params(),
        cost_estimate=pl.CostEstimate(
            flops=6 * 2 * volume.size * (lanes + 2 * rows),
            bytes_accessed=volume.size * 4 + rows * depth * lanes * 4,
            transcendentals=0,
        ),
        name="spectrum",
    )(me, volume, table_y, table_x, take_cosine, take_sine)


def middle(sources, dims, start, me, damping, matches, length_x, tables):
    slabs, submaps, _, depth, lanes = dims
    length_z = slabs * depth
    slots = len(sources)
    size = math.prod(dims)
    scratch = [
        pltpu.VMEM((6, submaps, length_z, lanes), F32),
        pltpu.VMEM((submaps, length_z, lanes), F32),
        wide_scratch(tables[0]),
        wide_scratch(tables[1]),
    ]
    if slots > 1:
        scratch.append(pltpu.VMEM((size // lanes, lanes), F32))
    return pl.pallas_call(
        functools.partial(cross_kernel, length_x, dims),
        out_shape=[jax.ShapeDtypeStruct(part.shape, F32) for part in sources],
        in_specs=[scalar_spec()] * 4 + [whole_spec()] * (slots + 2),
        out_specs=[whole_spec()] * slots,
        scratch_shapes=scratch,
        compiler_params=params(),
        cost_estimate=pl.CostEstimate(
            flops=6 * 2 * size * length_z * 2, bytes_accessed=size * 8, transcendentals=size
        ),
        name="middle",
    )(start, me, damping, matches, *sources, *tables)


def inverse(columns, me, before, length, tables):
    slots = len(columns)
    depth, each, lanes = columns[0].shape[-3:]
    weights = tables[0]
    rows = weights.shape[0]
    width = math.gcd(depth, WIDTH)
    block = pl.BlockSpec((width, length, lanes), lambda g: (g, 0, 0))
    if slots == 1:
        source = pl.BlockSpec((rows // each, width, each, lanes), lambda g: (0, g, 0, 0))
    else:
        source = pl.BlockSpec((width, each, lanes), lambda g: (g, 0, 0))
    extra = [] if before is None else [before]
    return pl.pallas_call(
        functools.partial(inverse_kernel, rows, slots, len(extra)),
        out_shape=jax.ShapeDtypeStruct((depth, length, lanes), F32),
        grid=(depth // width,),
        in_specs=[scalar_spec()] + [source] * slots + [whole_spec()] * 3 + [block] * len(extra),
        out_specs=block,
        scratch_shapes=[wide_scratch(tables[1])]
        + ([pltpu.VMEM((2, slots, each, lanes), F32)] if slots > 1 else []),
        compiler_params=params(),
        cost_estimate=pl.CostEstimate(
            flops=6 * 2 * depth * length * lanes * rows,
            bytes_accessed=rows * depth * lanes * 4 + depth * length * lanes * 4 * (1 + len(extra)),
            transcendentals=0,
        ),
        name="inverse",
    )(me, *columns, *tables, *extra)


def ends(size):
    up = [(i, i + 1) for i in range(size - 1)]
    return up, [(j, i) for i, j in up]


def diffuse_plain(field, classes, conductance):
    up, down = ends(lax.axis_size("slab"))

    def widened(volume):
        before = lax.ppermute(volume[-1:], "slab", up)
        after = lax.ppermute(volume[:1], "slab", down)
        return jnp.pad(jnp.concatenate([before, volume, after], axis=0), ((0, 0), (1, 1), (1, 1)))

    def around(volume):
        wide = widened(volume)
        core = slice(1, -1)
        for low in (slice(2, None), slice(None, -2)):
            yield wide[low, core, core]
            yield wide[core, low, core]
            yield wide[core, core, low]

    kappa = conductance[classes]
    others = list(around(kappa))
    for _ in range(STEPS):
        change = jnp.zeros_like(field)
        for near, beside in zip(around(field), others):
            change = change + 0.5 * (kappa + beside) * (near - field)
        field = field + STEP_SIZE * change
    return field


def local(occupancy, classes, conductance, damping, matches):
    slabs, pairs = lax.axis_size("slab"), lax.axis_size("pair")
    devices = slabs * pairs
    occ, cls = occupancy[0], classes[0]
    depth, length, lanes = occ.shape
    each = length // devices
    chunks = 2 if each % 2 == 0 else 1
    rows = each // chunks
    length_z = depth * slabs

    kx = np.arange(length)
    cos_x, sin_x = trig(kx, kx, length)
    take_cosine, take_sine, weights = first_column_masks(kx, length, lanes)
    table_y = right_table(half_forward(lanes))
    kz = np.arange(length_z)
    cos_z, sin_z = trig(kz, kz, length_z)
    middle_tables = (left_table_stack(cos_z, sin_z), left_table(np.concatenate([cos_z, sin_z], axis=1)))
    table_back = right_table(half_inverse(lanes))

    if depth >= 4 * STEPS:
        up, down = ends(slabs)
        pack = lambda low, high: jnp.concatenate([occ[low:high], cls[low:high].astype(F32)], axis=0)
        below = lax.ppermute(pack(depth - STEPS, depth), "slab", up)
        above = lax.ppermute(pack(0, STEPS), "slab", down)
        at = lax.axis_index("slab")
        edge = jnp.stack([at > 0, at < slabs - 1]).astype(jnp.int32)
        inner = diffuse_inner(occ, cls, conductance)
        volume = diffuse_outer(occ, cls, conductance, edge, below, above, inner)
    else:
        volume = diffuse_plain(occ, cls, conductance)

    me = lax.axis_index(AXES).astype(jnp.int32).reshape(1)
    straight = depth % 8 == 0
    span = length // chunks

    def turns(chunk):
        return chunk % 2 == 1 and rows % 8 == 0 and devices <= MOST_TURNS

    def exchange(parts):
        if len(parts) == 1:
            return [lax.all_to_all(parts[0], AXES, 0, 0, tiled=True)]
        moved = [parts[0]]
        for slot in range(1, devices):
            pairs_of = [(i, (i + slot) % devices) for i in range(devices)]
            moved.append(lax.ppermute(parts[slot], AXES, pairs_of))
        return moved

    dims = (slabs, pairs, rows, depth, lanes)
    backs = []
    for chunk in range(chunks):
        inside = slice(chunk * span, (chunk + 1) * span)
        table_x = left_table_stack(cos_x[inside], sin_x[inside])
        slots = devices if turns(chunk) else 1
        tables = (table_y, table_x, take_cosine[inside], take_sine[inside])
        parts = spectrum(volume, me, devices, slots, tables)
        parts = exchange(parts)
        shapes, shape = [part.shape for part in parts], dims
        if not straight:
            parts = [parts[0].reshape(slabs, pairs, depth, rows, lanes).transpose(1, 0, 2, 3, 4)]
            shape = (1, pairs, rows, length_z, lanes)
        parts = [part.reshape(-1, lanes) for part in parts]
        start = chunk * span + me * rows
        parts = middle(parts, shape, start, me, damping, matches, length, middle_tables)
        if not straight:
            parts = [parts[0].reshape(pairs, slabs, depth, rows, lanes).transpose(1, 0, 2, 3, 4)]
        backs.append([part.reshape(like) for part, like in zip(parts, shapes)])
    result = None
    for chunk in range(chunks):
        parts = exchange(backs[chunk])
        inside = slice(chunk * span, (chunk + 1) * span)
        table = left_table(np.concatenate([cos_x[:, inside], sin_x[:, inside]], axis=1))
        result = inverse(parts, me, result, length, (weights[inside], table, table_back))
    return result[None]


def left_table_stack(cosine, sine):
    return np.concatenate([left_table(cosine), left_table(sine)], axis=0)


def solution(mesh):
    in_specs = (
        P(("groups", "pair"), "slab", None, None),
        P(("groups", "pair"), "slab", None, None),
        P(),
        P("groups"),
        P("groups"),
    )
    out_specs = P(("groups", "pair"), "slab", None, None)

    return jax.shard_map(local, mesh=mesh, in_specs=in_specs, out_specs=out_specs, check_vma=False)
```
